32 devices in a mesh: rep: 2 (over y), chol: 8 (over z, x), pop: 2 (over core).
Axes of the slice: x: 2, y: 2, z: 4, core: 2. Of those that a mesh axis runs over, the one named last changes fastest.
Arguments:
- green_half: bfloat16 [256, 16, 1024], P(('rep', 'chol'), 'pop'), parts along dimension 0, may hold values from -5 to 5
- step_delta: bfloat16 [256, 16, 1024], P(('rep', 'chol'), 'pop'), parts along dimension 0, may hold values from -4 to 4
- chol_vectors: bfloat16 [96, 128, 1024], P(('rep', 'chol')), parts along dimension 0, as said below
- copy_counts: int32 [32], P(('rep', 'pop')), parts along dimension 0, may hold values from 0 to 2, as said below
- parents: int32 [32], P('rep'), parts along dimension 0, may hold values from 0 to 15, as said below
Outputs:
- parent_force: bfloat16 [256, 16, 1024], P(('rep', 'chol'), 'pop'), parts along dimension 0
- child_energy: float32 [32], P(('rep', 'pop')), parts along dimension 0
The draws below stay inside these ranges and needn't reach their ends.
There are 2 independent parts, one for each index of `rep`. The reference program is written for one: setup_inputs(seed, part) draws one part's arguments, and reference() takes and returns one part's arrays. A program takes and returns all parts, laid end to end along the dimension named above; each array names one. Nothing has to cross between parts.
Inputs may be any that keep to these rules, and one draw needn't show every extreme that they name: copy_counts[p] is the number of children c with parents[c] = p; the counts sum to 16; some walker has 0 copies and some has 2. parents never falls from one child to the next; the first child's parent is walker 0 and the last child's is walker 16 - 1; each child's parent is the child itself or a walker next to it. `chol_vectors`: entries are of order 1 / sqrt(1024) times a factor per vector.
All inputs are finite; a program needn't handle non-finite values.
Results may differ from the reference program's by a relative error of at most 0.0057.
Values may be sent and summed in bfloat16 or wider, within the bound.
No kernel may reach another device: no remote copies, remote signals or barrier semaphores. Data moves between devices by JAX's collectives and lax.ppermute only.
A program may use at most 64 MiB of HBM per device.

```python
import math
import jax
import jax.numpy as jnp
from jax import lax

NOCC = 128
NBASIS = 1024
CHOL_DEV = 6
NCHOL = 48
WALKERS = 16
N_CHOL = 8


def draw_green_half(key, part):
    folded = jax.random.fold_in(key, 11)
    key_values, key_rows, key_columns = jax.random.split(folded, 3)
    dims_all = (NOCC, WALKERS, NBASIS)
    values = jax.random.truncated_normal(key_values, -4.0, 4.0, dims_all, jnp.float32)
    row_lower = 0.03
    row_upper = 0.3
    column_lower = 0.3
    column_upper = 3.0
    row_scale = jnp.exp(jax.random.uniform(key_rows, (NOCC, WALKERS, 1), jnp.float32, math.log(row_lower), math.log(row_upper)))
    column_scale = jnp.exp(jax.random.uniform(key_columns, (1, WALKERS, NBASIS), jnp.float32, math.log(column_lower), math.log(column_upper)))
    return (values * row_scale * column_scale).astype(jnp.bfloat16)


def draw_chol_vectors(key, part):
    folded = jax.random.fold_in(key, 23)
    key_values, key_rough = jax.random.split(folded)
    dims_all = (NCHOL, NOCC, NBASIS)
    position = jnp.arange(NCHOL, dtype=jnp.float32) / (NCHOL - 1)
    rough = jnp.exp(jax.random.uniform(key_rough, (NCHOL,), jnp.float32, math.log(0.7), math.log(1.4)))
    ramp = jnp.exp(position * math.log(3.0)) * rough
    values = jax.random.truncated_normal(key_values, -4.0, 4.0, dims_all, jnp.float32)
    return (values * ramp[:, None, None] / NBASIS ** 0.5).astype(jnp.bfloat16)


def resample(key):
    folded = jax.random.fold_in(key, 5)
    key_offset, key_picks, key_which, key_forced = jax.random.split(folded, 4)
    half_count = WALKERS // 2
    offset = jax.random.randint(key_offset, (), 0, 2, dtype=jnp.int32)
    pairs_live = ((WALKERS - offset) // 2).astype(jnp.int32)
    picks = jax.random.randint(key_picks, (half_count,), 0, 3, dtype=jnp.int32)
    chosen = jax.random.randint(key_which, (), 0, pairs_live, dtype=jnp.int32)
    forced = jax.random.randint(key_forced, (), 1, 3, dtype=jnp.int32)
    pair_index = jnp.arange(half_count, dtype=jnp.int32)
    picks = jnp.where(pair_index == chosen, forced, picks).astype(jnp.int32)
    pair_first = (offset + 2 * pair_index).astype(jnp.int32)
    picks = jnp.where((pair_first == 0) & (picks == 2), 1, picks).astype(jnp.int32)
    picks = jnp.where((pair_first + 1 == WALKERS - 1) & (picks == 1), 2, picks).astype(jnp.int32)
    walker_ids = jnp.arange(WALKERS, dtype=jnp.int32)
    shifted = (walker_ids - offset).astype(jnp.int32)
    pair_ids = jnp.floor_divide(shifted, 2).astype(jnp.int32)
    live = (shifted >= 0) & (pair_ids < pairs_live)
    safe_ids = jnp.clip(pair_ids, 0, half_count - 1).astype(jnp.int32)
    pair_pick = jnp.take(picks, safe_ids)
    start_of = (offset + 2 * safe_ids).astype(jnp.int32)
    parent_ids = jnp.where(pair_pick == 1, start_of, jnp.where(pair_pick == 2, start_of + 1, walker_ids))
    parent_ids = jnp.where(live, parent_ids, walker_ids).astype(jnp.int32)
    counts = jnp.sum((parent_ids[:, None] == walker_ids[None, :]).astype(jnp.int32), axis=0)
    return (counts.astype(jnp.int32), parent_ids)


def draw_copy_counts(key, part):
    return resample(key)[0]


def draw_parents(key, part):
    return resample(key)[1]


def shard_levels(key, dims, shards, low, largest):
    gain = 1.0
    for dim, blocks in shards:
        draws = jax.random.uniform(jax.random.fold_in(jax.random.fold_in(key, 6), dim), (blocks,), jnp.float32, low / len(shards), largest / len(shards))
        gain = gain * jnp.repeat(jnp.exp(draws), dims[dim] // blocks).reshape((-1,) + (1,) * (len(dims) - 1 - dim))
    return gain


def gaussian(rng, shape, width, most, shards=(), kind=jnp.bfloat16):
    array = jax.random.normal(rng, shape, jnp.float32) * width
    if len(shards) > 0:
        array = shard_levels(rng, shape, shards, -0.22, 0.18) * array
    return jnp.clip(array, min=-most, max=most).astype(kind)


def setup_inputs(seed: int = 0, part: int = 0) -> dict:
    splits = jax.random.split(jax.random.key(seed), 6)
    part_splits = jax.random.split(jax.random.fold_in(splits[5], part), 6)
    green_half = draw_green_half(jax.random.fold_in(jax.random.fold_in(splits[5], part), 71), part)
    step_delta = gaussian(part_splits[1], (NOCC, WALKERS, NBASIS), 0.5, 4.0, ((0, 8), (1, 2)))
    chol_vectors = draw_chol_vectors(jax.random.fold_in(jax.random.fold_in(splits[5], part), 71), part)
    copy_counts = draw_copy_counts(jax.random.fold_in(jax.random.fold_in(splits[5], part), 71), part)
    parents = draw_parents(jax.random.fold_in(jax.random.fold_in(splits[5], part), 71), part)
    return {"green_half": green_half, "step_delta": step_delta, "chol_vectors": chol_vectors, "copy_counts": copy_counts, "parents": parents}


def reference(green_half, step_delta, chol_vectors, copy_counts, parents):
    picked = jnp.take(green_half, parents, axis=1).astype(jnp.float32)
    child_rows = (picked + step_delta.astype(jnp.float32)).astype(jnp.bfloat16)
    child_wide = child_rows.astype(jnp.float32)
    factor = -1.0 / (NCHOL ** 0.5)
    chol_blocks = chol_vectors.reshape(N_CHOL, CHOL_DEV, NOCC, NBASIS)

    def accumulate(state_pair, chol_block):
        force_sum, traces = state_pair
        vectors = chol_block.astype(jnp.float32)
        cross = jnp.einsum("iwm,gkm->wgik", child_wide, vectors, precision=lax.Precision.HIGHEST)
        cross_low = lax.optimization_barrier(cross.astype(jnp.bfloat16)).astype(jnp.float32)
        force_sum = force_sum + factor * jnp.einsum("wgik,gil->kwl", cross_low, vectors, precision=lax.Precision.HIGHEST)
        traces = traces + jnp.sum(cross_low * jnp.swapaxes(cross, 2, 3), axis=(1, 2, 3))
        return (force_sum, traces), None

    start_state = (jnp.zeros((NOCC, WALKERS, NBASIS), jnp.float32), jnp.zeros((WALKERS,), jnp.float32))
    final_state, unused = lax.scan(accumulate, start_state, chol_blocks)
    force_sum, traces = final_state
    child_energy = (-0.125 / (NCHOL * NOCC)) * traces
    one_hot = (parents[:, None] == jnp.arange(WALKERS, dtype=jnp.int32)[None, :]).astype(jnp.float32)
    summed = jnp.einsum("kcl,cp->kpl", force_sum, one_hot, precision=lax.Precision.HIGHEST)
    divisor = jnp.maximum(copy_counts, 1).astype(jnp.float32)
    return (summed / divisor[None, :, None]).astype(jnp.bfloat16), child_energy
```

```python
import functools

import jax
import jax.numpy as jnp
from jax import lax
from jax.experimental import pallas as pl
from jax.experimental.pallas import tpu as pltpu
from jax.sharding import PartitionSpec as P

F32 = jnp.float32
BF16 = jnp.bfloat16
VMEM = pl.BlockSpec(memory_space=pltpu.VMEM)
SMEM = pl.BlockSpec(memory_space=pltpu.SMEM)


def plain_shards(green_half, step_delta, chol_vectors, copy_counts, parents):
    per_group = green_half.shape[1]
    total_chol = lax.axis_size("chol") * chol_vectors.shape[0]
    orbitals = chol_vectors.shape[1]
    factor = -1.0 / total_chol**0.5
    all_parents = lax.all_gather(green_half, "pop", axis=1, tiled=True)
    my_parents = lax.dynamic_slice_in_dim(parents, lax.axis_index("pop") * per_group, per_group, 0)
    picked = jnp.take(all_parents, my_parents, axis=1)
    child_rows = (picked.astype(F32) + step_delta.astype(F32)).astype(BF16)
    cross = jnp.einsum(
        "iwm,gkm->wgik",
        lax.all_gather(child_rows, "chol", axis=0, tiled=True),
        chol_vectors,
        preferred_element_type=F32,
    )
    cross_low = cross.astype(BF16)
    trace_part = jnp.sum(cross_low.astype(F32) * jnp.swapaxes(cross, 2, 3), axis=(1, 2, 3))
    child_energy = lax.psum(trace_part, "chol") * (-0.125 / (total_chol * orbitals))
    forces = lax.psum_scatter(
        factor * jnp.einsum("wgik,gil->kwl", cross_low, chol_vectors, preferred_element_type=F32),
        "chol",
        scatter_dimension=0,
        tiled=True,
    )
    parent_slots = jnp.arange(all_parents.shape[1], dtype=jnp.int32)
    one_hot = (my_parents[:, None] == parent_slots[None, :]).astype(F32)
    spread_sum = jnp.einsum("kcl,cp->kpl", forces, one_hot, precision=lax.Precision.HIGHEST)
    summed = lax.psum_scatter(
        spread_sum.astype(BF16), "pop", scatter_dimension=1, tiled=True
    ).astype(F32)
    divisor = jnp.maximum(copy_counts, 1).astype(F32)
    return (summed / divisor[None, :, None]).astype(BF16), child_energy


def ring_device(n, place):
    return place * 2 if place < n // 2 else 2 * (n - 1 - place) + 1


def ring_pairs(n, step):
    return [(ring_device(n, q), ring_device(n, (q + step) % n)) for q in range(n)]


def block_at(n, offset):
    me = lax.axis_index("chol")
    place = jnp.where(lax.rem(me, 2) == 0, me // 2, n - 1 - me // 2)
    place = lax.rem(place + offset, n)
    return jnp.where(place < n // 2, 2 * place, 2 * (n - 1 - place) + 1)


def group_base(group, walkers, size):
    mine = lax.axis_index("pop")
    first = mine * (walkers - size)
    return first if group == 0 else (walkers - size) - first


def child_kernel(group, size, parents_ref, green_ref, delta_ref, *refs):
    if group == 1:
        other_ref, out_ref, green_wide, delta_wide, other_wide = refs
    else:
        out_ref, green_wide, delta_wide = refs
    rows, walkers, width = green_ref.shape
    mine = lax.axis_index("pop")
    base = group_base(group, walkers, size)
    for t in range(width // 128):
        lanes = slice(t * 128, t * 128 + 128)
        green_wide[t] = green_ref[:, :, lanes].astype(F32).reshape(rows * walkers, 128)
        delta_wide[t] = delta_ref[:, :, lanes].astype(F32).reshape(rows * walkers, 128)
        if group == 1:
            other_wide[t] = other_ref[:, :, lanes].astype(F32).reshape(rows * walkers, 128)
    edge = jnp.where(mine == 0, 0, walkers - 1)
    for j in range(size):
        walker = base + j
        parent = parents_ref[mine * walkers + walker] - mine * walkers
        inside = jnp.logical_and(parent >= 0, parent < walkers)
        source = jnp.clip(parent, 0, walkers - 1)
        for t in range(width // 128):
            picked = green_wide[t, pl.ds(source, rows, stride=walkers), :]
            if group == 1:
                outer = other_wide[t, pl.ds(edge, rows, stride=walkers), :]
                picked = jnp.where(inside, picked, outer)
            change = delta_wide[t, pl.ds(walker, rows, stride=walkers), :]
            out_ref[j, :, t * 128 : t * 128 + 128] = (picked + change).astype(BF16)


def make_children(group, size, parents, green, delta, other=None):
    rows, walkers, width = green.shape
    operands = (parents, green, delta) + ((other,) if group == 1 else ())
    return pl.pallas_call(
        functools.partial(child_kernel, group, size),
        out_shape=jax.ShapeDtypeStruct((size, rows, width), BF16),
        in_specs=[SMEM] + [VMEM] * (len(operands) - 1),
        out_specs=VMEM,
        scratch_shapes=[pltpu.VMEM((width // 128, rows * walkers, 128), F32)] * (2 + group),
        cost_estimate=pl.CostEstimate(
            flops=green.size, bytes_accessed=6 * green.size, transcendentals=0
        ),
        name=f"children{group}",
    )(*operands)


def force_kernel(group, walkers, factor, energy_scale, n, *refs):
    chol_ref, chunks, rest = refs[0], refs[1 : n + 1], refs[n + 1 :]
    energy_in = rest[0] if group == 1 else None
    outs = rest[group : group + n]
    energy_ref, child, low, force = rest[group + n :]
    size, rows, width = chunks[0].shape
    vectors, orbitals, _ = chol_ref.shape
    starts = [pl.multiple_of(block_at(n, r) * rows, rows) for r in range(n)]
    for c in range(size):
        for r in range(n):
            child[c, pl.ds(starts[r], rows), :] = chunks[r][c]
    chol = chol_ref[...].reshape(vectors * orbitals, width)
    step = 2 if size % 2 == 0 else 1
    for c in range(0, size, step):
        cross = lax.dot_general(
            chol,
            child[c : c + step].reshape(step * orbitals, width),
            (((1,), (1,)), ((), ())),
            preferred_element_type=F32,
        ).astype(BF16)
        for d in range(step):
            for g in range(vectors):
                low[c + d, :, g * orbitals : (g + 1) * orbitals] = cross[
                    g * orbitals : (g + 1) * orbitals, d * orbitals : (d + 1) * orbitals
                ]
    force[...] = jnp.dot(
        low[...].reshape(size * orbitals, vectors * orbitals), chol, preferred_element_type=F32
    ).reshape(size, orbitals, width)
    for r in range(n):
        for c in range(size):
            outs[r][c] = (force[c, pl.ds(starts[r], rows), :] * factor).astype(outs[r].dtype)
    base = group_base(group, walkers, size)
    slot = lax.broadcasted_iota(jnp.int32, (walkers, 128), 0)
    energy = energy_in[...] if group == 1 else jnp.zeros((walkers, 128), F32)
    for c in range(size):
        product = jnp.sum(child[c].astype(F32) * force[c], axis=0, keepdims=True)
        lanes = sum(product[:, s : s + 128] for s in range(0, width, 128))
        energy = energy + jnp.where(slot == base + c, lanes * energy_scale, 0.0)
    energy_ref[...] = energy


def partial_forces(group, walkers, chol, chunks, energy=None):
    n = len(chunks)
    size, rows, width = chunks[0].shape
    vectors, orbitals, _ = chol.shape
    total = n * vectors
    extra = (energy,) if group == 1 else ()
    shape = (size, rows, width)
    return pl.pallas_call(
        functools.partial(
            force_kernel,
            group,
            walkers,
            -1.0 / total**0.5,
            -0.125 / (total * orbitals),
            n,
        ),
        out_shape=[jax.ShapeDtypeStruct(shape, F32)]
        + [jax.ShapeDtypeStruct(shape, BF16)] * (n - 1)
        + [jax.ShapeDtypeStruct((walkers, 128), F32)],
        in_specs=[VMEM] * (1 + n + len(extra)),
        out_specs=[VMEM] * (n + 1),
        scratch_shapes=[
            pltpu.VMEM((size, orbitals, width), BF16),
            pltpu.VMEM((size, orbitals, vectors * orbitals), BF16),
            pltpu.VMEM((size, orbitals, width), F32),
        ],
        cost_estimate=pl.CostEstimate(
            flops=4 * size * orbitals * width * vectors * orbitals,
            bytes_accessed=2 * chol.size + 4 * size * orbitals * width,
            transcendentals=0,
        ),
        name=f"forces{group}",
    )(chol, *chunks, *extra)


def parent_kernel(size, parents_ref, counts_ref, edge_ref, *refs):
    groups = (refs[0:3], refs[3:6])
    out_ref, total, spread = refs[6:]
    rows, walkers, width = out_ref.shape
    mine = lax.axis_index("pop")
    for group, (own, up, down) in enumerate(groups):
        base = group_base(group, walkers, size)
        for j in range(size):
            total[base + j] = own[j] + up[j].astype(F32) + down[j].astype(F32)
    edge = edge_ref[...].astype(F32)
    for p in range(walkers):
        parent = mine * walkers + p
        summed = jnp.zeros((rows, width), F32)
        for c in range(max(p - 1, 0), min(p + 2, walkers)):
            hit = parents_ref[mine * walkers + c] == parent
            summed = summed + jnp.where(hit, total[c], 0.0)
        if p in (0, walkers - 1):
            child = parent + (1 if p else -1)
            valid = jnp.logical_and(child >= 0, child < parents_ref.shape[0])
            found = parents_ref[jnp.clip(child, 0, parents_ref.shape[0] - 1)] == parent
            summed = summed + jnp.where(jnp.logical_and(valid, found), edge, 0.0)
        divisor = jnp.maximum(counts_ref[p], 1).astype(F32)
        mean = summed / divisor
        for t in range(width // 128):
            spread[t, pl.ds(p, rows, stride=walkers), :] = mean[:, t * 128 : t * 128 + 128]
    for t in range(width // 128):
        block = spread[t].astype(BF16).reshape(rows, walkers, 128)
        out_ref[:, :, t * 128 : t * 128 + 128] = block


def parent_forces(parents, counts, edge, group_a, group_b):
    size, rows, width = group_a[0].shape
    walkers = counts.shape[0]
    return pl.pallas_call(
        functools.partial(parent_kernel, size),
        out_shape=jax.ShapeDtypeStruct((rows, walkers, width), BF16),
        in_specs=[SMEM, SMEM] + [VMEM] * 7,
        out_specs=VMEM,
        scratch_shapes=[
            pltpu.VMEM((walkers, rows, width), F32),
            pltpu.VMEM((width // 128, rows * walkers, 128), F32),
        ],
        cost_estimate=pl.CostEstimate(
            flops=6 * rows * walkers * width,
            bytes_accessed=10 * rows * walkers * width,
            transcendentals=0,
        ),
        name="parents",
    )(parents, counts, edge, *group_a, *group_b)


def swap_cores(x):
    return lax.ppermute(x, "pop", [(0, 1), (1, 0)])


def add_low(own, received):
    return (own.astype(F32) + received.astype(F32)).astype(BF16)


def ring_shards(green_half, step_delta, chol_vectors, copy_counts, parents):
    n = lax.axis_size("chol")
    rows, walkers, width = green_half.shape
    size = walkers // 2
    up, down = ring_pairs(n, 1), ring_pairs(n, -1)
    ups = (n // 2, n - 1 - n // 2)
    downs = (n - 1 - n // 2, n // 2)

    other = swap_cores(green_half)
    own = [
        make_children(0, size, parents, green_half, step_delta),
        make_children(1, size, parents, green_half, step_delta, other),
    ]
    chunks = [[own[g]] + [None] * (n - 1) for g in (0, 1)]
    for s in range(1, n // 2 + 1):
        for g in (0, 1):
            if s <= ups[g]:
                chunks[g][n - s] = lax.ppermute(chunks[g][(n - s + 1) % n], "chol", up)
            if s <= downs[g]:
                chunks[g][s] = lax.ppermute(chunks[g][s - 1], "chol", down)

    *parts_a, energy = partial_forces(0, walkers, chol_vectors, chunks[0])
    *parts_b, energy = partial_forces(1, walkers, chol_vectors, chunks[1], energy)
    parts = (parts_a, parts_b)

    rising, falling = [None, None], [None, None]
    for s in range(1, n // 2 + 1):
        for g in (0, 1):
            if s <= ups[g]:
                send = parts[g][ups[g] - s + 1]
                if s > 1:
                    send = add_low(send, rising[g])
                rising[g] = lax.ppermute(send, "chol", up)
            if s <= downs[g]:
                send = parts[g][n - (downs[g] - s + 1)]
                if s > 1:
                    send = add_low(send, falling[g])
                falling[g] = lax.ppermute(send, "chol", down)

    span = 1
    while span < n:
        energy = energy + lax.ppermute(energy, "chol", [(i, i ^ span) for i in range(n)])
        span *= 2

    at = (size - 1) * (1 - lax.axis_index("pop"))
    row = [lax.dynamic_index_in_dim(a, at, 0, keepdims=False).astype(F32)
           for a in (parts[1][0], rising[1], falling[1])]
    edge = swap_cores((row[0] + row[1] + row[2]).astype(BF16))
    parent_force = parent_forces(
        parents,
        copy_counts,
        edge,
        (parts[0][0], rising[0], falling[0]),
        (parts[1][0], rising[1], falling[1]),
    )
    return parent_force, jnp.sum(energy, axis=1)


def shards(green_half, step_delta, chol_vectors, copy_counts, parents):
    rows, walkers, _ = green_half.shape
    n = lax.axis_size("chol")
    tiles = rows % 16 == 0 and walkers % 8 == 0 and n & (n - 1) == 0 and n >= 4
    run = ring_shards if tiles and lax.axis_size("pop") == 2 else plain_shards
    return run(green_half, step_delta, chol_vectors, copy_counts, parents)


def solution(mesh):
    placed = (
        P(("rep", "chol"), "pop", None),
        P(("rep", "chol"), "pop", None),
        P(("rep", "chol"), None, None),
        P(("rep", "pop")),
        P("rep"),
    )
    return jax.shard_map(
        shards,
        mesh=mesh,
        in_specs=placed,
        out_specs=(P(("rep", "chol"), "pop", None), P(("rep", "pop"))),
        check_vma=False,
    )
```

```python
import functools

import jax
import jax.numpy as jnp
from jax import lax
from jax.experimental import pallas as pl
from jax.experimental.pallas import tpu as pltpu
from jax.sharding import PartitionSpec as P


F32 = jnp.float32
BF16 = jnp.bfloat16
VMEM = pl.BlockSpec(memory_space=pltpu.VMEM)
SMEM = pl.BlockSpec(memory_space=pltpu.SMEM)


def plain_shards(green_half, step_delta, chol_vectors, copy_counts, parents):
    per_group = green_half.shape[1]
    total_chol = lax.axis_size("chol") * chol_vectors.shape[0]
    orbitals = chol_vectors.shape[1]
    factor = -1.0 / total_chol**0.5
    all_parents = lax.all_gather(green_half, "pop", axis=1, tiled=True)
    my_parents = lax.dynamic_slice_in_dim(parents, lax.axis_index("pop") * per_group, per_group, 0)
    picked = jnp.take(all_parents, my_parents, axis=1)
    child_rows = (picked.astype(F32) + step_delta.astype(F32)).astype(BF16)
    cross = jnp.einsum(
        "iwm,gkm->wgik",
        lax.all_gather(child_rows, "chol", axis=0, tiled=True),
        chol_vectors,
        preferred_element_type=F32,
    )
    cross_low = cross.astype(BF16)
    trace_part = jnp.sum(cross_low.astype(F32) * jnp.swapaxes(cross, 2, 3), axis=(1, 2, 3))
    child_energy = lax.psum(trace_part, "chol") * (-0.125 / (total_chol * orbitals))
    forces = lax.psum_scatter(
        factor * jnp.einsum("wgik,gil->kwl", cross_low, chol_vectors, preferred_element_type=F32),
        "chol",
        scatter_dimension=0,
        tiled=True,
    )
    parent_slots = jnp.arange(all_parents.shape[1], dtype=jnp.int32)
    one_hot = (my_parents[:, None] == parent_slots[None, :]).astype(F32)
    spread_sum = jnp.einsum("kcl,cp->kpl", forces, one_hot, precision=lax.Precision.HIGHEST)
    summed = lax.psum_scatter(
        spread_sum.astype(BF16), "pop", scatter_dimension=1, tiled=True
    ).astype(F32)
    divisor = jnp.maximum(copy_counts, 1).astype(F32)
    return (summed / divisor[None, :, None]).astype(BF16), child_energy


def ring_device(n, place):
    return place * 2 if place < n // 2 else 2 * (n - 1 - place) + 1


def ring_pairs(n, step):
    return [(ring_device(n, q), ring_device(n, (q + step) % n)) for q in range(n)]


def block_at(n, offset):
    me = lax.axis_index("chol")
    place = jnp.where(lax.rem(me, 2) == 0, me // 2, n - 1 - me // 2)
    place = lax.rem(place + offset, n)
    return jnp.where(place < n // 2, 2 * place, 2 * (n - 1 - place) + 1)


def group_base(group, walkers, size):
    mine = lax.axis_index("pop")
    first = mine * (walkers - size)
    return first if group == 0 else (walkers - size) - first


def child_kernel(group, size, parents_ref, green_ref, delta_ref, *refs):
    if group == 1:
        other_ref, out_ref, green_wide, delta_wide, other_wide = refs
    else:
        out_ref, green_wide, delta_wide = refs
    rows, walkers, width = green_ref.shape
    mine = lax.axis_index("pop")
    base = group_base(group, walkers, size)
    for t in range(width // 128):
        lanes = slice(t * 128, t * 128 + 128)
        green_wide[t] = green_ref[:, :, lanes].astype(F32).reshape(rows * walkers, 128)
        delta_wide[t] = delta_ref[:, :, lanes].astype(F32).reshape(rows * walkers, 128)
        if group == 1:
            other_wide[t] = other_ref[:, :, lanes].astype(F32).reshape(rows * walkers, 128)
    edge = jnp.where(mine == 0, 0, walkers - 1)
    for j in range(size):
        walker = base + j
        parent = parents_ref[mine * walkers + walker] - mine * walkers
        inside = jnp.logical_and(parent >= 0, parent < walkers)
        source = jnp.clip(parent, 0, walkers - 1)
        for t in range(width // 128):
            picked = green_wide[t, pl.ds(source, rows, stride=walkers), :]
            if group == 1:
                outer = other_wide[t, pl.ds(edge, rows, stride=walkers), :]
                picked = jnp.where(inside, picked, outer)
            change = delta_wide[t, pl.ds(walker, rows, stride=walkers), :]
            out_ref[j, :, t * 128 : t * 128 + 128] = (picked + change).astype(BF16)


def make_children(group, size, parents, green, delta, other=None):
    rows, walkers, width = green.shape
    operands = (parents, green, delta) + ((other,) if group == 1 else ())
    return pl.pallas_call(
        functools.partial(child_kernel, group, size),
        out_shape=jax.ShapeDtypeStruct((size, rows, width), BF16),
        in_specs=[SMEM] + [VMEM] * (len(operands) - 1),
        out_specs=VMEM,
        scratch_shapes=[pltpu.VMEM((width // 128, rows * walkers, 128), F32)] * (2 + group),
        cost_estimate=pl.CostEstimate(
            flops=green.size, bytes_accessed=6 * green.size, transcendentals=0
        ),
        compiler_params=pltpu.CompilerParams(vmem_limit_bytes=6 << 20),
    )(*operands)


def force_kernel(group, walkers, factor, energy_scale, n, *refs):
    chol_ref, chunks, rest = refs[0], refs[1 : n + 1], refs[n + 1 :]
    energy_in = rest[0] if group == 1 else None
    outs = rest[group : group + n]
    energy_ref, child, low, force = rest[group + n :]
    size, rows, width = chunks[0].shape
    vectors, orbitals, _ = chol_ref.shape
    starts = [pl.multiple_of(block_at(n, r) * rows, rows) for r in range(n)]
    for c in range(size):
        for r in range(n):
            child[c, pl.ds(starts[r], rows), :] = chunks[r][c]
    chol = chol_ref[...].reshape(vectors * orbitals, width)
    step = 2 if size % 2 == 0 else 1
    for c in range(0, size, step):
        cross = lax.dot_general(
            chol,
            child[c : c + step].reshape(step * orbitals, width),
            (((1,), (1,)), ((), ())),
            preferred_element_type=F32,
        ).astype(BF16)
        for d in range(step):
            for g in range(vectors):
                low[c + d, :, g * orbitals : (g + 1) * orbitals] = cross[
                    g * orbitals : (g + 1) * orbitals, d * orbitals : (d + 1) * orbitals
                ]
    force[...] = jnp.dot(
        low[...].reshape(size * orbitals, vectors * orbitals), chol, preferred_element_type=F32
    ).reshape(size, orbitals, width)
    for r in range(n):
        for c in range(size):
            outs[r][c] = (force[c, pl.ds(starts[r], rows), :] * factor).astype(outs[r].dtype)
    base = group_base(group, walkers, size)
    slot = lax.broadcasted_iota(jnp.int32, (walkers, 128), 0)
    energy = energy_in[...] if group == 1 else jnp.zeros((walkers, 128), F32)
    for c in range(size):
        product = jnp.sum(child[c].astype(F32) * force[c], axis=0, keepdims=True)
        lanes = sum(product[:, s : s + 128] for s in range(0, width, 128))
        energy = energy + jnp.where(slot == base + c, lanes * energy_scale, 0.0)
    energy_ref[...] = energy


def partial_forces(group, walkers, chol, chunks, energy=None):
    n = len(chunks)
    size, rows, width = chunks[0].shape
    vectors, orbitals, _ = chol.shape
    total = n * vectors
    extra = (energy,) if group == 1 else ()
    shape = (size, rows, width)
    return pl.pallas_call(
        functools.partial(
            force_kernel,
            group,
            walkers,
            -1.0 / total**0.5,
            -0.125 / (total * orbitals),
            n,
        ),
        out_shape=[jax.ShapeDtypeStruct(shape, F32)]
        + [jax.ShapeDtypeStruct(shape, BF16)] * (n - 1)
        + [jax.ShapeDtypeStruct((walkers, 128), F32)],
        in_specs=[VMEM] * (1 + n + len(extra)),
        out_specs=[VMEM] * (n + 1),
        scratch_shapes=[
            pltpu.VMEM((size, orbitals, width), BF16),
            pltpu.VMEM((size, orbitals, vectors * orbitals), BF16),
            pltpu.VMEM((size, orbitals, width), F32),
        ],
        cost_estimate=pl.CostEstimate(
            flops=4 * size * orbitals * width * vectors * orbitals,
            bytes_accessed=2 * chol.size + 4 * size * orbitals * width,
            transcendentals=0,
        ),
        compiler_params=pltpu.CompilerParams(vmem_limit_bytes=16 << 20),
    )(chol, *chunks, *extra)


def parent_kernel(size, parents_ref, counts_ref, edge_ref, *refs):
    groups = (refs[0:3], refs[3:6])
    out_ref, total, spread = refs[6:]
    rows, walkers, width = out_ref.shape
    mine = lax.axis_index("pop")
    for group, (own, up, down) in enumerate(groups):
        base = group_base(group, walkers, size)
        for j in range(size):
            total[base + j] = own[j] + up[j].astype(F32) + down[j].astype(F32)
    edge = edge_ref[...].astype(F32)
    for p in range(walkers):
        parent = mine * walkers + p
        summed = jnp.zeros((rows, width), F32)
        for c in range(max(p - 1, 0), min(p + 2, walkers)):
            hit = parents_ref[mine * walkers + c] == parent
            summed = summed + jnp.where(hit, total[c], 0.0)
        if p in (0, walkers - 1):
            child = parent + (1 if p else -1)
            valid = jnp.logical_and(child >= 0, child < parents_ref.shape[0])
            found = parents_ref[jnp.clip(child, 0, parents_ref.shape[0] - 1)] == parent
            summed = summed + jnp.where(jnp.logical_and(valid, found), edge, 0.0)
        divisor = jnp.maximum(counts_ref[p], 1).astype(F32)
        mean = summed / divisor
        for t in range(width // 128):
            spread[t, pl.ds(p, rows, stride=walkers), :] = mean[:, t * 128 : t * 128 + 128]
    for t in range(width // 128):
        block = spread[t].astype(BF16).reshape(rows, walkers, 128)
        out_ref[:, :, t * 128 : t * 128 + 128] = block


def parent_forces(parents, counts, edge, group_a, group_b):
    size, rows, width = group_a[0].shape
    walkers = counts.shape[0]
    return pl.pallas_call(
        functools.partial(parent_kernel, size),
        out_shape=jax.ShapeDtypeStruct((rows, walkers, width), BF16),
        in_specs=[SMEM, SMEM] + [VMEM] * 7,
        out_specs=VMEM,
        scratch_shapes=[
            pltpu.VMEM((walkers, rows, width), F32),
            pltpu.VMEM((width // 128, rows * walkers, 128), F32),
        ],
        cost_estimate=pl.CostEstimate(
            flops=6 * rows * walkers * width,
            bytes_accessed=10 * rows * walkers * width,
            transcendentals=0,
        ),
        compiler_params=pltpu.CompilerParams(vmem_limit_bytes=6 << 20),
        name="parents",
    )(parents, counts, edge, *group_a, *group_b)


def swap_cores(x):
    return lax.ppermute(x, "pop", [(0, 1), (1, 0)])


def add_low(own, received):
    return (own.astype(F32) + received.astype(F32)).astype(BF16)


def hop_order(n):
    longer = (("up", "down"), ("down", "up"))
    order = []
    for phase in ("gather", "sum"):
        for s in range(1, n // 2 + 1):
            for g in (0, 1):
                for way in ("up", "down"):
                    if s < n // 2 or way == longer[g][0]:
                        order.append((phase, s, g, way))
    return order


def ring_shards(green_half, step_delta, chol_vectors, copy_counts, parents):
    n = lax.axis_size("chol")
    _, walkers, _ = green_half.shape
    size = walkers // 2
    pairs = {"up": ring_pairs(n, 1), "down": ring_pairs(n, -1)}
    hops = ({"up": n // 2, "down": n // 2 - 1}, {"up": n // 2 - 1, "down": n // 2})

    def hop(x, key):
        return lax.ppermute(x, "chol", pairs[key[3]])

    other = swap_cores(green_half)
    own = [
        make_children(0, size, parents, green_half, step_delta),
        make_children(1, size, parents, green_half, step_delta, other),
    ]
    chunks = [[own[g]] + [None] * (n - 1) for g in (0, 1)]
    parts = [None, None]
    arrived = [{}, {}]
    for key in hop_order(n):
        phase, s, g, way = key
        if phase == "gather":
            here, there = (n - s, (n - s + 1) % n) if way == "up" else (s, s - 1)
            chunks[g][here] = hop(chunks[g][there], key)
            continue
        if parts[g] is None:
            extra = () if g == 0 else (energy,)
            *parts[g], energy = partial_forces(g, walkers, chol_vectors, chunks[g], *extra)
        left = hops[g][way] - s + 1
        send = parts[g][left if way == "up" else n - left]
        if s > 1:
            send = add_low(send, arrived[g][way])
        arrived[g][way] = hop(send, key)

    span = 1
    while span < n:
        energy = energy + lax.ppermute(energy, "chol", [(i, i ^ span) for i in range(n)])
        span *= 2

    at = (size - 1) * (1 - lax.axis_index("pop"))
    last = (parts[1][0], arrived[1]["up"], arrived[1]["down"])
    row = [lax.dynamic_index_in_dim(a, at, 0, keepdims=False).astype(F32) for a in last]
    edge = swap_cores((row[0] + row[1] + row[2]).astype(BF16))
    first = (parts[0][0], arrived[0]["up"], arrived[0]["down"])
    parent_force = parent_forces(parents, copy_counts, edge, first, last)
    return parent_force, jnp.sum(energy, axis=1)


def on_ring(n, pops, rows, walkers):
    return rows % 16 == 0 and walkers % 8 == 0 and n & (n - 1) == 0 and n >= 4 and pops == 2


def shards(green_half, step_delta, chol_vectors, copy_counts, parents):
    rows, walkers, _ = green_half.shape
    if on_ring(lax.axis_size("chol"), lax.axis_size("pop"), rows, walkers):
        return ring_shards(green_half, step_delta, chol_vectors, copy_counts, parents)
    return plain_shards(green_half, step_delta, chol_vectors, copy_counts, parents)


def solution(mesh):
    placed = (
        P(("rep", "chol"), "pop", None),
        P(("rep", "chol"), "pop", None),
        P(("rep", "chol"), None, None),
        P(("rep", "pop")),
        P("rep"),
    )
    step = jax.shard_map(
        shards,
        mesh=mesh,
        in_specs=placed,
        out_specs=(P(("rep", "chol"), "pop", None), P(("rep", "pop"))),
        check_vma=False,
    )

    def run(green_half, step_delta, chol_vectors, copy_counts, parents):
        given = (green_half, step_delta, chol_vectors, copy_counts, parents)
        return step(*given)

    return run
```

```python
import functools

import jax
import jax.numpy as jnp
from jax import lax
from jax.experimental import pallas as pl
from jax.experimental.pallas import tpu as pltpu
from jax.sharding import PartitionSpec as P


F32 = jnp.float32
BF16 = jnp.bfloat16
VMEM = pl.BlockSpec(memory_space=pltpu.VMEM)
SMEM = pl.BlockSpec(memory_space=pltpu.SMEM)


def plain_shards(green_half, step_delta, chol_vectors, copy_counts, parents):
    per_group = green_half.shape[1]
    total_chol = lax.axis_size("chol") * chol_vectors.shape[0]
    orbitals = chol_vectors.shape[1]
    factor = -1.0 / total_chol**0.5
    all_parents = lax.all_gather(green_half, "pop", axis=1, tiled=True)
    my_parents = lax.dynamic_slice_in_dim(parents, lax.axis_index("pop") * per_group, per_group, 0)
    picked = jnp.take(all_parents, my_parents, axis=1)
    child_rows = (picked.astype(F32) + step_delta.astype(F32)).astype(BF16)
    cross = jnp.einsum(
        "iwm,gkm->wgik",
        lax.all_gather(child_rows, "chol", axis=0, tiled=True),
        chol_vectors,
        preferred_element_type=F32,
    )
    cross_low = cross.astype(BF16)
    trace_part = jnp.sum(cross_low.astype(F32) * jnp.swapaxes(cross, 2, 3), axis=(1, 2, 3))
    child_energy = lax.psum(trace_part, "chol") * (-0.125 / (total_chol * orbitals))
    forces = lax.psum_scatter(
        factor * jnp.einsum("wgik,gil->kwl", cross_low, chol_vectors, preferred_element_type=F32),
        "chol",
        scatter_dimension=0,
        tiled=True,
    )
    parent_slots = jnp.arange(all_parents.shape[1], dtype=jnp.int32)
    one_hot = (my_parents[:, None] == parent_slots[None, :]).astype(F32)
    spread_sum = jnp.einsum("kcl,cp->kpl", forces, one_hot, precision=lax.Precision.HIGHEST)
    summed = lax.psum_scatter(
        spread_sum.astype(BF16), "pop", scatter_dimension=1, tiled=True
    ).astype(F32)
    divisor = jnp.maximum(copy_counts, 1).astype(F32)
    return (summed / divisor[None, :, None]).astype(BF16), child_energy


def ring_device(n, place):
    return place * 2 if place < n // 2 else 2 * (n - 1 - place) + 1


def ring_pairs(n, step):
    return [(ring_device(n, q), ring_device(n, (q + step) % n)) for q in range(n)]


def block_at(n, offset):
    me = lax.axis_index("chol")
    place = jnp.where(lax.rem(me, 2) == 0, me // 2, n - 1 - me // 2)
    place = lax.rem(place + offset, n)
    return jnp.where(place < n // 2, 2 * place, 2 * (n - 1 - place) + 1)


def group_base(group, walkers, size):
    first = lax.axis_index("pop") * (walkers - size)
    return (walkers - size) - first if group == 0 else first


def message_rows(size, rows, width):
    return size * rows * (width // 128) + 8


def message_block(c, t, rows, width):
    first = (c * (width // 128) + t) * rows
    return slice(first, first + rows)


def children_kernel(parents_any, green_any, delta_any, other_ref, out0_ref, out1_ref, *scratch):
    parents_ref, green_ref, delta_ref, green_wide, delta_wide, other_wide, sems = scratch
    rows, walkers, width = green_ref.shape
    copies = [
        pltpu.make_async_copy(source, target, sems.at[k])
        for k, (source, target) in enumerate(
            ((parents_any, parents_ref), (green_any, green_ref), (delta_any, delta_ref))
        )
    ]
    for copy in copies:
        copy.start()
    mine = lax.axis_index("pop")
    blocks = [slice(t * 128, t * 128 + 128) for t in range(width // 128)]
    for t, lanes in enumerate(blocks):
        other_wide[t] = other_ref[:, :, lanes].astype(F32).reshape(rows * walkers, 128)
    for copy in copies:
        copy.wait()
    for t, lanes in enumerate(blocks):
        green_wide[t] = green_ref[:, :, lanes].astype(F32).reshape(rows * walkers, 128)
        delta_wide[t] = delta_ref[:, :, lanes].astype(F32).reshape(rows * walkers, 128)
    edge = jnp.where(mine == 0, 0, walkers - 1)
    for group, out_ref in enumerate((out0_ref, out1_ref)):
        size = out_ref.shape[0]
        base = group_base(group, walkers, size)
        for j in range(size):
            walker = base + j
            parent = parents_ref[mine * walkers + walker] - mine * walkers
            inside = jnp.logical_and(parent >= 0, parent < walkers)
            source = jnp.clip(parent, 0, walkers - 1)
            for t, lanes in enumerate(blocks):
                picked = green_wide[t, pl.ds(source, rows, stride=walkers), :]
                if group == 0:
                    outer = other_wide[t, pl.ds(edge, rows, stride=walkers), :]
                    picked = jnp.where(inside, picked, outer)
                change = delta_wide[t, pl.ds(walker, rows, stride=walkers), :]
                out_ref[j, :, lanes] = (picked + change).astype(BF16)


def make_children(size, parents, green, delta, other):
    rows, walkers, width = green.shape
    wide = pltpu.VMEM((width // 128, rows * walkers, 128), F32)
    return pl.pallas_call(
        children_kernel,
        out_shape=[
            jax.ShapeDtypeStruct((size, rows, width), BF16),
            jax.ShapeDtypeStruct((walkers - size, rows, width), BF16),
        ],
        in_specs=[pl.BlockSpec(memory_space=pltpu.HBM)] * 3 + [VMEM],
        out_specs=[VMEM, VMEM],
        scratch_shapes=[
            pltpu.SMEM(parents.shape, jnp.int32),
            pltpu.VMEM(green.shape, BF16),
            pltpu.VMEM(delta.shape, BF16),
            wide,
            wide,
            wide,
            pltpu.SemaphoreType.DMA((3,)),
        ],
        cost_estimate=pl.CostEstimate(
            flops=green.size, bytes_accessed=6 * green.size, transcendentals=0
        ),
        compiler_params=pltpu.CompilerParams(vmem_limit_bytes=8 << 20),
        name="children",
    )(parents, green, delta, other)


def force_kernel(factor, energy_scale, n, *refs):
    chol_ref, chunks, outs = refs[0], refs[1 : n + 1], refs[n + 1 : 2 * n + 1]
    child, low, force = refs[2 * n + 1 :]
    size, rows, width = chunks[0].shape
    vectors, orbitals, _ = chol_ref.shape
    starts = [pl.multiple_of(block_at(n, r) * rows, rows) for r in range(n)]
    for c in range(size):
        for r in range(n):
            child[c, pl.ds(starts[r], rows), :] = chunks[r][c]
    chol = chol_ref[...].reshape(vectors * orbitals, width)
    step = 2 if size % 2 == 0 else 1
    for c in range(0, size, step):
        cross = lax.dot_general(
            chol,
            child[c : c + step].reshape(step * orbitals, width),
            (((1,), (1,)), ((), ())),
            preferred_element_type=F32,
        ).astype(BF16)
        for d in range(step):
            for g in range(vectors):
                low[c + d, :, g * orbitals : (g + 1) * orbitals] = cross[
                    g * orbitals : (g + 1) * orbitals, d * orbitals : (d + 1) * orbitals
                ]
    force[...] = jnp.dot(
        low[...].reshape(size * orbitals, vectors * orbitals), chol, preferred_element_type=F32
    ).reshape(size, orbitals, width)
    sums = []
    for c in range(size):
        product = jnp.sum(child[c].astype(F32) * force[c], axis=0, keepdims=True)
        sums.append(sum(product[:, s : s + 128] for s in range(0, width, 128)))
    sums = jnp.concatenate(sums + [jnp.zeros((8 - size, 128), F32)], axis=0)
    energy = jnp.sum(sums, axis=1, keepdims=True) * energy_scale
    high = energy.astype(BF16).astype(F32)
    lane = lax.broadcasted_iota(jnp.int32, (8, 128), 1) - 2 * lax.axis_index("chol")
    tile = jnp.where(lane == 0, high, 0.0) + jnp.where(lane == 1, energy - high, 0.0)
    for r in range(n):
        for c in range(size):
            for t in range(width // 128):
                block = force[c, pl.ds(starts[r], rows), t * 128 : t * 128 + 128]
                outs[r][message_block(c, t, rows, width), :] = (block * factor).astype(
                    outs[r].dtype
                )
        outs[r][message_rows(size, rows, width) - 8 :, :] = tile.astype(outs[r].dtype)


def partial_forces(chol, chunks):
    n = len(chunks)
    size, rows, width = chunks[0].shape
    vectors, orbitals, _ = chol.shape
    total = n * vectors
    shape = (message_rows(size, rows, width), 128)
    return pl.pallas_call(
        functools.partial(
            force_kernel, -1.0 / total**0.5, -0.125 / (total * orbitals), n
        ),
        out_shape=[jax.ShapeDtypeStruct(shape, F32)]
        + [jax.ShapeDtypeStruct(shape, BF16)] * (n - 1),
        in_specs=[VMEM] * (1 + n),
        out_specs=[VMEM] * n,
        scratch_shapes=[
            pltpu.VMEM((size, orbitals, width), BF16),
            pltpu.VMEM((size, orbitals, vectors * orbitals), BF16),
            pltpu.VMEM((size, orbitals, width), F32),
        ],
        cost_estimate=pl.CostEstimate(
            flops=4 * size * orbitals * width * vectors * orbitals,
            bytes_accessed=2 * chol.size + 4 * size * orbitals * width,
            transcendentals=0,
        ),
        compiler_params=pltpu.CompilerParams(vmem_limit_bytes=16 << 20),
    )(chol, *chunks)


def parents_kernel(size, parents_ref, counts_ref, edge_ref, *refs):
    groups = (refs[0:3], refs[3:6])
    out_ref, energy_ref, total, spread = refs[6:]
    rows, walkers, width = out_ref.shape
    blocks = width // 128
    mine = lax.axis_index("pop")
    row = lax.broadcasted_iota(jnp.int32, (8, 128), 0)
    lane = lax.broadcasted_iota(jnp.int32, (8, 128), 1)
    energies = jnp.zeros((1, 128), F32)
    for group, (own, up, down) in enumerate(groups):
        base = group_base(group, walkers, size)
        for j in range(size):
            span = slice(j * blocks * rows, (j + 1) * blocks * rows)
            total[base + j] = own[span, :] + up[span, :].astype(F32) + down[span, :].astype(F32)
        tail = slice(size * blocks * rows, size * blocks * rows + 8)
        halves = own[tail, :] + up[tail, :].astype(F32) + down[tail, :].astype(F32)
        column = jnp.sum(halves, axis=1, keepdims=True)
        here = jnp.logical_and(lane == row + base, row < size)
        energies = energies + jnp.sum(jnp.where(here, column, 0.0), axis=0, keepdims=True)
    energy_ref[...] = energies[:, :walkers]
    edge = edge_ref[...].astype(F32)
    last = parents_ref.shape[0] - 1
    for p in range(walkers):
        parent = mine * walkers + p
        summed = jnp.zeros((blocks * rows, 128), F32)
        for c in range(max(p - 1, 0), min(p + 2, walkers)):
            hit = parents_ref[mine * walkers + c] == parent
            summed = summed + jnp.where(hit, total[c], 0.0)
        if p in (0, walkers - 1):
            child = parent + (1 if p else -1)
            valid = jnp.logical_and(child >= 0, child <= last)
            found = parents_ref[jnp.clip(child, 0, last)] == parent
            summed = summed + jnp.where(jnp.logical_and(valid, found), edge, 0.0)
        mean = summed * (1.0 / jnp.maximum(counts_ref[p], 1).astype(F32))
        for t in range(blocks):
            spread[t, pl.ds(p, rows, stride=walkers), :] = mean[t * rows : (t + 1) * rows, :]
    for t in range(blocks):
        block = spread[t].astype(BF16).reshape(rows, walkers, 128)
        out_ref[:, :, t * 128 : t * 128 + 128] = block


def parent_forces(shape, size, parents, counts, edge, group0, group1):
    rows, walkers, width = shape
    return pl.pallas_call(
        functools.partial(parents_kernel, size),
        out_shape=[
            jax.ShapeDtypeStruct(shape, BF16),
            jax.ShapeDtypeStruct((1, walkers), F32),
        ],
        in_specs=[SMEM, SMEM] + [VMEM] * 7,
        out_specs=[VMEM, VMEM],
        scratch_shapes=[
            pltpu.VMEM((walkers, rows * width // 128, 128), F32),
            pltpu.VMEM((width // 128, rows * walkers, 128), F32),
        ],
        cost_estimate=pl.CostEstimate(
            flops=6 * rows * walkers * width,
            bytes_accessed=10 * rows * walkers * width,
            transcendentals=0,
        ),
        compiler_params=pltpu.CompilerParams(vmem_limit_bytes=6 << 20),
        name="parents",
    )(parents, counts, edge, *group0, *group1)


def swap_cores(x):
    return lax.ppermute(x, "pop", [(0, 1), (1, 0)])


def add_low(own, received):
    return (own.astype(F32) + received.astype(F32)).astype(BF16)


def hop_order(n):
    half = n // 2
    order = [("gather", 1, 0, "up"), ("gather", 1, 1, "down")]
    for s in range(1, half):
        order += [("gather", s, 0, "down"), ("gather", s + 1, 0, "up")]
        order += [("gather", s, 1, "up"), ("gather", s + 1, 1, "down")]
    for s in range(1, half):
        order += [("sum", s, g, way) for g in (0, 1) for way in ("up", "down")]
    return order + [("sum", half, 0, "up"), ("sum", half, 1, "down")]


def ring_shards(green_half, step_delta, chol_vectors, copy_counts, parents):
    n = lax.axis_size("chol")
    rows, walkers, width = green_half.shape
    size = walkers // 2
    pairs = {"up": ring_pairs(n, 1), "down": ring_pairs(n, -1)}
    hops = ({"up": n // 2, "down": n // 2 - 1}, {"up": n // 2 - 1, "down": n // 2})

    def hop(x, key):
        return lax.ppermute(x, "chol", pairs[key[3]])

    other = swap_cores(green_half)
    own = make_children(size, parents, green_half, step_delta, other)
    chunks = [[own[g]] + [None] * (n - 1) for g in (0, 1)]
    parts = [None, None]
    arrived = [{}, {}]
    for key in hop_order(n):
        phase, s, g, way = key
        if phase == "gather":
            here, there = (n - s, (n - s + 1) % n) if way == "up" else (s, s - 1)
            chunks[g][here] = hop(chunks[g][there], key)
            continue
        if parts[g] is None:
            parts[g] = partial_forces(chol_vectors, chunks[g])
        left = hops[g][way] - s + 1
        send = parts[g][left if way == "up" else n - left]
        if s > 1:
            send = add_low(send, arrived[g][way])
        arrived[g][way] = hop(send, key)

    group0, group1 = [(parts[g][0], arrived[g]["up"], arrived[g]["down"]) for g in (0, 1)]
    per_walker = rows * width // 128
    at = (size - 1) * (1 - lax.axis_index("pop")) * per_walker
    own, up, down = [
        lax.dynamic_slice_in_dim(a, at, per_walker, 0).astype(F32) for a in group0
    ]
    edge = swap_cores((own + up + down).astype(BF16))
    parent_force, energy = parent_forces(
        green_half.shape, size, parents, copy_counts, edge, group0, group1
    )
    return parent_force, energy.reshape(walkers)


def on_ring(n, pops, rows, walkers):
    whole_tiles = rows % 16 == 0 and walkers % 8 == 0 and walkers <= 16
    return whole_tiles and n & (n - 1) == 0 and 4 <= n <= 64 and pops == 2


def shards(green_half, step_delta, chol_vectors, copy_counts, parents):
    rows, walkers, _ = green_half.shape
    if on_ring(lax.axis_size("chol"), lax.axis_size("pop"), rows, walkers):
        return ring_shards(green_half, step_delta, chol_vectors, copy_counts, parents)
    return plain_shards(green_half, step_delta, chol_vectors, copy_counts, parents)


def solution(mesh):
    placed = (
        P(("rep", "chol"), "pop", None),
        P(("rep", "chol"), "pop", None),
        P(("rep", "chol"), None, None),
        P(("rep", "pop")),
        P("rep"),
    )
    step = jax.shard_map(
        shards,
        mesh=mesh,
        in_specs=placed,
        out_specs=(P(("rep", "chol"), "pop", None), P(("rep", "pop"))),
        check_vma=False,
    )

    def run(green_half, step_delta, chol_vectors, copy_counts, parents):
        given = (green_half, step_delta, chol_vectors, copy_counts, parents)
        return step(*given)

    return run
```

```python
import functools

import jax
import jax.numpy as jnp
from jax import lax
from jax.experimental import pallas as pl
from jax.experimental.pallas import tpu as pltpu
from jax.sharding import PartitionSpec as P


F32 = jnp.float32
BF16 = jnp.bfloat16
VMEM = pl.BlockSpec(memory_space=pltpu.VMEM)
SMEM = pl.BlockSpec(memory_space=pltpu.SMEM)


def plain_shards(green_half, step_delta, chol_vectors, copy_counts, parents):
    per_group = green_half.shape[1]
    total_chol = lax.axis_size("chol") * chol_vectors.shape[0]
    orbitals = chol_vectors.shape[1]
    factor = -1.0 / total_chol**0.5
    all_parents = lax.all_gather(green_half, "pop", axis=1, tiled=True)
    my_parents = lax.dynamic_slice_in_dim(parents, lax.axis_index("pop") * per_group, per_group, 0)
    picked = jnp.take(all_parents, my_parents, axis=1)
    child_rows = (picked.astype(F32) + step_delta.astype(F32)).astype(BF16)
    cross = jnp.einsum(
        "iwm,gkm->wgik",
        lax.all_gather(child_rows, "chol", axis=0, tiled=True),
        chol_vectors,
        preferred_element_type=F32,
    )
    cross_low = cross.astype(BF16)
    trace_part = jnp.sum(cross_low.astype(F32) * jnp.swapaxes(cross, 2, 3), axis=(1, 2, 3))
    child_energy = lax.psum(trace_part, "chol") * (-0.125 / (total_chol * orbitals))
    forces = lax.psum_scatter(
        factor * jnp.einsum("wgik,gil->kwl", cross_low, chol_vectors, preferred_element_type=F32),
        "chol",
        scatter_dimension=0,
        tiled=True,
    )
    parent_slots = jnp.arange(all_parents.shape[1], dtype=jnp.int32)
    one_hot = (my_parents[:, None] == parent_slots[None, :]).astype(F32)
    spread_sum = jnp.einsum("kcl,cp->kpl", forces, one_hot, precision=lax.Precision.HIGHEST)
    summed = lax.psum_scatter(
        spread_sum.astype(BF16), "pop", scatter_dimension=1, tiled=True
    ).astype(F32)
    divisor = jnp.maximum(copy_counts, 1).astype(F32)
    return (summed / divisor[None, :, None]).astype(BF16), child_energy


def ring_device(n, place):
    return place * 2 if place < n // 2 else 2 * (n - 1 - place) + 1


def ring_pairs(n, step):
    return [(ring_device(n, q), ring_device(n, (q + step) % n)) for q in range(n)]


def block_at(n, offset):
    me = lax.axis_index("chol")
    place = jnp.where(lax.rem(me, 2) == 0, me // 2, n - 1 - me // 2)
    place = lax.rem(place + offset, n)
    return jnp.where(place < n // 2, 2 * place, 2 * (n - 1 - place) + 1)


def group_base(group, walkers, size):
    first = lax.axis_index("pop") * (walkers - size)
    return (walkers - size) - first if group == 0 else first


def message_rows(size, rows, width):
    return size * rows * (width // 128) + 8


def message_block(c, t, rows, width):
    first = (c * (width // 128) + t) * rows
    return slice(first, first + rows)


def children_kernel(parents_any, green_any, delta_any, chol_any, *refs):
    out0_ref, out1_ref, chol_ref, change_ref, outside_ref = refs[:5]
    parents_ref, green_ref, delta_ref, green_wide, delta_wide, sems = refs[5:]
    rows, walkers, width = green_ref.shape
    copies = [
        pltpu.make_async_copy(source, target, sems.at[k])
        for k, (source, target) in enumerate(
            (
                (parents_any, parents_ref),
                (green_any, green_ref),
                (delta_any, delta_ref),
                (chol_any, chol_ref),
            )
        )
    ]
    for copy in copies:
        copy.start()
    for copy in copies[:3]:
        copy.wait()
    mine = lax.axis_index("pop")
    blocks = [slice(t * 128, t * 128 + 128) for t in range(width // 128)]
    for t, lanes in enumerate(blocks):
        green_wide[t] = green_ref[:, :, lanes].astype(F32).reshape(rows * walkers, 128)
        delta_wide[t] = delta_ref[:, :, lanes].astype(F32).reshape(rows * walkers, 128)

    def local_parent(walker):
        return parents_ref[mine * walkers + walker] - mine * walkers

    for group, out_ref in enumerate((out0_ref, out1_ref)):
        size = out_ref.shape[0]
        base = group_base(group, walkers, size)
        for j in range(size):
            walker = base + j
            source = jnp.clip(local_parent(walker), 0, walkers - 1)
            for t, lanes in enumerate(blocks):
                picked = green_wide[t, pl.ds(source, rows, stride=walkers), :]
                change = delta_wide[t, pl.ds(walker, rows, stride=walkers), :]
                out_ref[j, :, lanes] = (picked + change).astype(BF16)
    child = edge_walker(walkers)
    for t, lanes in enumerate(blocks):
        change_ref[:, lanes] = delta_wide[t, pl.ds(child, rows, stride=walkers), :]
    parent = local_parent(child)
    outside = jnp.where(jnp.logical_or(parent < 0, parent >= walkers), 1.0, 0.0)
    outside_ref[...] = jnp.full((rows, 128), outside, F32)
    copies[3].wait()


def edge_walker(walkers):
    return jnp.where(lax.axis_index("pop") == 0, walkers - 1, 0)


def edge_kernel(chunk_ref, change_ref, outside_ref, other_ref, out_ref, other_wide):
    size, rows, width = out_ref.shape
    walkers = other_ref.shape[1]
    j = jnp.where(lax.axis_index("pop") == 0, size - 1, 0)
    row = walkers - 1 - edge_walker(walkers)
    outside = outside_ref[...] > 0.5
    out_ref[...] = chunk_ref[...]
    for t in range(width // 128):
        lanes = slice(t * 128, t * 128 + 128)
        other_wide[t] = other_ref[:, :, lanes].astype(F32).reshape(rows * walkers, 128)
        picked = other_wide[t, pl.ds(row, rows, stride=walkers), :]
        moved = picked + change_ref[:, lanes]
        kept = chunk_ref[j, :, lanes].astype(F32)
        out_ref[j, :, lanes] = jnp.where(outside, moved, kept).astype(BF16)


def make_children(size, parents, green, delta, chol):
    rows, walkers, width = green.shape
    wide = pltpu.VMEM((width // 128, rows * walkers, 128), F32)
    here = [
        pltpu.with_memory_space_constraint(a, pltpu.HBM) for a in (parents, green, delta, chol)
    ]
    return pl.pallas_call(
        children_kernel,
        out_shape=[
            jax.ShapeDtypeStruct((size, rows, width), BF16),
            jax.ShapeDtypeStruct((walkers - size, rows, width), BF16),
            jax.ShapeDtypeStruct(chol.shape, BF16),
            jax.ShapeDtypeStruct((rows, width), F32),
            jax.ShapeDtypeStruct((rows, 128), F32),
        ],
        in_specs=[pl.BlockSpec(memory_space=pltpu.HBM)] * 4,
        out_specs=[VMEM] * 5,
        scratch_shapes=[
            pltpu.SMEM(parents.shape, jnp.int32),
            pltpu.VMEM(green.shape, BF16),
            pltpu.VMEM(delta.shape, BF16),
            wide,
            wide,
            pltpu.SemaphoreType.DMA((4,)),
        ],
        cost_estimate=pl.CostEstimate(
            flops=green.size, bytes_accessed=6 * green.size, transcendentals=0
        ),
        compiler_params=pltpu.CompilerParams(vmem_limit_bytes=8 << 20),
        name="children",
    )(*here)


def finish_edge(chunk, change, outside, other):
    rows, walkers, width = other.shape
    return pl.pallas_call(
        edge_kernel,
        out_shape=jax.ShapeDtypeStruct(chunk.shape, BF16),
        in_specs=[VMEM] * 4,
        out_specs=VMEM,
        scratch_shapes=[pltpu.VMEM((width // 128, rows * walkers, 128), F32)],
        cost_estimate=pl.CostEstimate(
            flops=other.size, bytes_accessed=4 * other.size, transcendentals=0
        ),
        compiler_params=pltpu.CompilerParams(vmem_limit_bytes=4 << 20),
        name="edge",
    )(chunk, change, outside, other)


def force_kernel(factor, energy_scale, n, *refs):
    chol_ref, chunks, outs = refs[0], refs[1 : n + 1], refs[n + 1 : 2 * n + 1]
    child, low, force = refs[2 * n + 1 :]
    size, rows, width = chunks[0].shape
    vectors, orbitals, _ = chol_ref.shape
    starts = [pl.multiple_of(block_at(n, r) * rows, rows) for r in range(n)]
    for c in range(size):
        for r in range(n):
            child[c, pl.ds(starts[r], rows), :] = chunks[r][c]
    chol = chol_ref[...].reshape(vectors * orbitals, width)
    step = 2 if size % 2 == 0 else 1
    for c in range(0, size, step):
        cross = lax.dot_general(
            chol,
            child[c : c + step].reshape(step * orbitals, width),
            (((1,), (1,)), ((), ())),
            preferred_element_type=F32,
        ).astype(BF16)
        for d in range(step):
            for g in range(vectors):
                low[c + d, :, g * orbitals : (g + 1) * orbitals] = cross[
                    g * orbitals : (g + 1) * orbitals, d * orbitals : (d + 1) * orbitals
                ]
    force[...] = jnp.dot(
        low[...].reshape(size * orbitals, vectors * orbitals), chol, preferred_element_type=F32
    ).reshape(size, orbitals, width)
    sums = []
    for c in range(size):
        product = jnp.sum(child[c].astype(F32) * force[c], axis=0, keepdims=True)
        sums.append(sum(product[:, s : s + 128] for s in range(0, width, 128)))
    sums = jnp.concatenate(sums + [jnp.zeros((8 - size, 128), F32)], axis=0)
    energy = jnp.sum(sums, axis=1, keepdims=True) * energy_scale
    high = energy.astype(BF16).astype(F32)
    lane = lax.broadcasted_iota(jnp.int32, (8, 128), 1) - 2 * lax.axis_index("chol")
    tile = jnp.where(lane == 0, high, 0.0) + jnp.where(lane == 1, energy - high, 0.0)
    for r in range(n):
        for c in range(size):
            for t in range(width // 128):
                block = force[c, pl.ds(starts[r], rows), t * 128 : t * 128 + 128]
                outs[r][message_block(c, t, rows, width), :] = (block * factor).astype(
                    outs[r].dtype
                )
        outs[r][message_rows(size, rows, width) - 8 :, :] = tile.astype(outs[r].dtype)


def partial_forces(chol, chunks):
    n = len(chunks)
    size, rows, width = chunks[0].shape
    vectors, orbitals, _ = chol.shape
    total = n * vectors
    shape = (message_rows(size, rows, width), 128)
    return pl.pallas_call(
        functools.partial(
            force_kernel, -1.0 / total**0.5, -0.125 / (total * orbitals), n
        ),
        out_shape=[jax.ShapeDtypeStruct(shape, F32)]
        + [jax.ShapeDtypeStruct(shape, BF16)] * (n - 1),
        in_specs=[VMEM] * (1 + n),
        out_specs=[VMEM] * n,
        scratch_shapes=[
            pltpu.VMEM((size, orbitals, width), BF16),
            pltpu.VMEM((size, orbitals, vectors * orbitals), BF16),
            pltpu.VMEM((size, orbitals, width), F32),
        ],
        cost_estimate=pl.CostEstimate(
            flops=4 * size * orbitals * width * vectors * orbitals,
            bytes_accessed=2 * chol.size + 4 * size * orbitals * width,
            transcendentals=0,
        ),
        compiler_params=pltpu.CompilerParams(vmem_limit_bytes=16 << 20),
    )(chol, *chunks)


def parents_kernel(size, parents_ref, counts_ref, edge_ref, *refs):
    groups = (refs[0:3], refs[3:6])
    out_ref, energy_ref, total, spread = refs[6:]
    rows, walkers, width = out_ref.shape
    blocks = width // 128
    mine = lax.axis_index("pop")
    row = lax.broadcasted_iota(jnp.int32, (8, 128), 0)
    lane = lax.broadcasted_iota(jnp.int32, (8, 128), 1)
    energies = jnp.zeros((1, 128), F32)
    for group, (own, up, down) in enumerate(groups):
        base = group_base(group, walkers, size)
        for j in range(size):
            span = slice(j * blocks * rows, (j + 1) * blocks * rows)
            total[base + j] = own[span, :] + up[span, :].astype(F32) + down[span, :].astype(F32)
        tail = slice(size * blocks * rows, size * blocks * rows + 8)
        halves = own[tail, :] + up[tail, :].astype(F32) + down[tail, :].astype(F32)
        column = jnp.sum(halves, axis=1, keepdims=True)
        here = jnp.logical_and(lane == row + base, row < size)
        energies = energies + jnp.sum(jnp.where(here, column, 0.0), axis=0, keepdims=True)
    energy_ref[...] = energies[:, :walkers]
    edge = edge_ref[...].astype(F32)
    last = parents_ref.shape[0] - 1
    for p in range(walkers):
        parent = mine * walkers + p
        summed = jnp.zeros((blocks * rows, 128), F32)
        for c in range(max(p - 1, 0), min(p + 2, walkers)):
            hit = parents_ref[mine * walkers + c] == parent
            summed = summed + jnp.where(hit, total[c], 0.0)
        if p in (0, walkers - 1):
            child = parent + (1 if p else -1)
            valid = jnp.logical_and(child >= 0, child <= last)
            found = parents_ref[jnp.clip(child, 0, last)] == parent
            summed = summed + jnp.where(jnp.logical_and(valid, found), edge, 0.0)
        mean = summed * (1.0 / jnp.maximum(counts_ref[p], 1).astype(F32))
        for t in range(blocks):
            spread[t, pl.ds(p, rows, stride=walkers), :] = mean[t * rows : (t + 1) * rows, :]
    for t in range(blocks):
        block = spread[t].astype(BF16).reshape(rows, walkers, 128)
        out_ref[:, :, t * 128 : t * 128 + 128] = block


def parent_forces(shape, size, parents, counts, edge, group0, group1):
    rows, walkers, width = shape
    return pl.pallas_call(
        functools.partial(parents_kernel, size),
        out_shape=[
            jax.ShapeDtypeStruct(shape, BF16),
            jax.ShapeDtypeStruct((1, walkers), F32),
        ],
        in_specs=[SMEM, SMEM] + [VMEM] * 7,
        out_specs=[VMEM, VMEM],
        scratch_shapes=[
            pltpu.VMEM((walkers, rows * width // 128, 128), F32),
            pltpu.VMEM((width // 128, rows * walkers, 128), F32),
        ],
        cost_estimate=pl.CostEstimate(
            flops=6 * rows * walkers * width,
            bytes_accessed=10 * rows * walkers * width,
            transcendentals=0,
        ),
        compiler_params=pltpu.CompilerParams(vmem_limit_bytes=6 << 20),
        name="parents",
    )(parents, counts, edge, *group0, *group1)


def swap_cores(x):
    return lax.ppermute(x, "pop", [(0, 1), (1, 0)])


def add_low(own, received):
    return (own.astype(F32) + received.astype(F32)).astype(BF16)


def hop_order(n):
    half = n // 2
    order = []
    for s in range(1, half):
        order += [("gather", s, g, way) for g in (0, 1) for way in ("up", "down")]
    order += [("gather", half, 0, "up"), ("gather", half, 1, "down")]
    order += [("sum", 1, 0, "up"), ("sum", 1, 1, "down")]
    for s in range(1, half):
        order += [("sum", s + 1, 0, "up"), ("sum", s, 0, "down")]
        order += [("sum", s, 1, "up"), ("sum", s + 1, 1, "down")]
    return order


def ring_shards(green_half, step_delta, chol_vectors, copy_counts, parents):
    n = lax.axis_size("chol")
    rows, walkers, width = green_half.shape
    size = walkers // 2
    pairs = {"up": ring_pairs(n, 1), "down": ring_pairs(n, -1)}
    hops = ({"up": n // 2, "down": n // 2 - 1}, {"up": n // 2 - 1, "down": n // 2})

    def hop(x, key):
        return lax.ppermute(x, "chol", pairs[key[3]])

    other = swap_cores(green_half)
    *own, chol, change, outside = make_children(
        size, parents, green_half, step_delta, chol_vectors
    )
    own[0] = finish_edge(own[0], change, outside, other)
    chunks = [[own[g]] + [None] * (n - 1) for g in (0, 1)]
    parts = [None, None]
    arrived = [{}, {}]
    for key in hop_order(n):
        phase, s, g, way = key
        if phase == "gather":
            here, there = (n - s, (n - s + 1) % n) if way == "up" else (s, s - 1)
            chunks[g][here] = hop(chunks[g][there], key)
            continue
        if parts[g] is None:
            parts[g] = partial_forces(chol, chunks[g])
        left = hops[g][way] - s + 1
        send = parts[g][left if way == "up" else n - left]
        if s > 1:
            send = add_low(send, arrived[g][way])
        arrived[g][way] = hop(send, key)

    group0, group1 = [(parts[g][0], arrived[g]["up"], arrived[g]["down"]) for g in (0, 1)]
    per_walker = rows * width // 128
    at = (size - 1) * (1 - lax.axis_index("pop")) * per_walker
    own, up, down = [
        lax.dynamic_slice_in_dim(a, at, per_walker, 0).astype(F32) for a in group0
    ]
    edge = swap_cores((own + up + down).astype(BF16))
    parent_force, energy = parent_forces(
        green_half.shape, size, parents, copy_counts, edge, group0, group1
    )
    return parent_force, energy.reshape(walkers)


def on_ring(n, pops, rows, walkers):
    whole_tiles = rows % 16 == 0 and walkers % 8 == 0 and walkers <= 16
    return whole_tiles and n & (n - 1) == 0 and 4 <= n <= 64 and pops == 2


def shards(green_half, step_delta, chol_vectors, copy_counts, parents):
    rows, walkers, _ = green_half.shape
    if on_ring(lax.axis_size("chol"), lax.axis_size("pop"), rows, walkers):
        return ring_shards(green_half, step_delta, chol_vectors, copy_counts, parents)
    return plain_shards(green_half, step_delta, chol_vectors, copy_counts, parents)


def solution(mesh):
    placed = (
        P(("rep", "chol"), "pop", None),
        P(("rep", "chol"), "pop", None),
        P(("rep", "chol"), None, None),
        P(("rep", "pop")),
        P("rep"),
    )
    step = jax.shard_map(
        shards,
        mesh=mesh,
        in_specs=placed,
        out_specs=(P(("rep", "chol"), "pop", None), P(("rep", "pop"))),
        check_vma=False,
    )

    def run(green_half, step_delta, chol_vectors, copy_counts, parents):
        given = (green_half, step_delta, chol_vectors, copy_counts, parents)
        return step(*given)

    return run
```

```python
import functools

import jax
import jax.numpy as jnp
from jax import lax
from jax.experimental import pallas as pl
from jax.experimental.pallas import tpu as pltpu
from jax.sharding import PartitionSpec as P


F32 = jnp.float32
BF16 = jnp.bfloat16
VMEM = pl.BlockSpec(memory_space=pltpu.VMEM)
SMEM = pl.BlockSpec(memory_space=pltpu.SMEM)


def plain_shards(green_half, step_delta, chol_vectors, copy_counts, parents):
    per_group = green_half.shape[1]
    total_chol = lax.axis_size("chol") * chol_vectors.shape[0]
    orbitals = chol_vectors.shape[1]
    factor = -1.0 / total_chol**0.5
    all_parents = lax.all_gather(green_half, "pop", axis=1, tiled=True)
    my_parents = lax.dynamic_slice_in_dim(parents, lax.axis_index("pop") * per_group, per_group, 0)
    picked = jnp.take(all_parents, my_parents, axis=1)
    child_rows = (picked.astype(F32) + step_delta.astype(F32)).astype(BF16)
    cross = jnp.einsum(
        "iwm,gkm->wgik",
        lax.all_gather(child_rows, "chol", axis=0, tiled=True),
        chol_vectors,
        preferred_element_type=F32,
    )
    cross_low = cross.astype(BF16)
    trace_part = jnp.sum(cross_low.astype(F32) * jnp.swapaxes(cross, 2, 3), axis=(1, 2, 3))
    child_energy = lax.psum(trace_part, "chol") * (-0.125 / (total_chol * orbitals))
    forces = lax.psum_scatter(
        factor * jnp.einsum("wgik,gil->kwl", cross_low, chol_vectors, preferred_element_type=F32),
        "chol",
        scatter_dimension=0,
        tiled=True,
    )
    parent_slots = jnp.arange(all_parents.shape[1], dtype=jnp.int32)
    one_hot = (my_parents[:, None] == parent_slots[None, :]).astype(F32)
    spread_sum = jnp.einsum("kcl,cp->kpl", forces, one_hot, precision=lax.Precision.HIGHEST)
    summed = lax.psum_scatter(
        spread_sum.astype(BF16), "pop", scatter_dimension=1, tiled=True
    ).astype(F32)
    divisor = jnp.maximum(copy_counts, 1).astype(F32)
    return (summed / divisor[None, :, None]).astype(BF16), child_energy


def ring_device(n, place):
    return place * 2 if place < n // 2 else 2 * (n - 1 - place) + 1


def ring_pairs(n, step):
    return [(ring_device(n, q), ring_device(n, (q + step) % n)) for q in range(n)]


def block_at(n, offset):
    me = lax.axis_index("chol")
    place = jnp.where(lax.rem(me, 2) == 0, me // 2, n - 1 - me // 2)
    place = lax.rem(place + offset, n)
    return jnp.where(place < n // 2, 2 * place, 2 * (n - 1 - place) + 1)


def group_base(group, walkers, size):
    first = lax.axis_index("pop") * (walkers - size)
    return (walkers - size) - first if group == 0 else first


def message_rows(size, rows, width):
    return size * rows * (width // 128) + 8


def message_block(c, t, rows, width):
    first = (c * (width // 128) + t) * rows
    return slice(first, first + rows)


def children_kernel(n, parents_any, green_any, delta_any, chol_any, *refs):
    out0_ref, out1_ref, chol_ref, change_ref, outside_ref = refs[:5]
    parents_ref, green_ref, delta_ref, green_wide, delta_wide, sems = refs[5:]
    rows, walkers, width = green_ref.shape
    moves = [(parents_any, parents_ref), (green_any, green_ref), (delta_any, delta_ref)]
    for r in range(n):
        first = pl.multiple_of(block_at(n, r) * rows, rows)
        moves.append(
            (chol_any.at[:, pl.ds(first, rows), :], chol_ref.at[:, pl.ds(r * rows, rows), :])
        )
    copies = [
        pltpu.make_async_copy(source, target, sems.at[k])
        for k, (source, target) in enumerate(moves)
    ]
    for copy in copies:
        copy.start()
    for copy in copies[:3]:
        copy.wait()
    mine = lax.axis_index("pop")
    blocks = [slice(t * 128, t * 128 + 128) for t in range(width // 128)]
    for t, lanes in enumerate(blocks):
        green_wide[t] = green_ref[:, :, lanes].astype(F32).reshape(rows * walkers, 128)
        delta_wide[t] = delta_ref[:, :, lanes].astype(F32).reshape(rows * walkers, 128)

    def local_parent(walker):
        return parents_ref[mine * walkers + walker] - mine * walkers

    for group, out_ref in enumerate((out0_ref, out1_ref)):
        size = out_ref.shape[0]
        base = group_base(group, walkers, size)
        for j in range(size):
            walker = base + j
            source = jnp.clip(local_parent(walker), 0, walkers - 1)
            for t, lanes in enumerate(blocks):
                picked = green_wide[t, pl.ds(source, rows, stride=walkers), :]
                change = delta_wide[t, pl.ds(walker, rows, stride=walkers), :]
                out_ref[j, :, lanes] = (picked + change).astype(BF16)
    child = edge_walker(walkers)
    for t, lanes in enumerate(blocks):
        change_ref[:, lanes] = delta_wide[t, pl.ds(child, rows, stride=walkers), :]
    parent = local_parent(child)
    outside = jnp.where(jnp.logical_or(parent < 0, parent >= walkers), 1.0, 0.0)
    outside_ref[...] = jnp.full((rows, 128), outside, F32)
    for copy in copies[3:]:
        copy.wait()


def edge_walker(walkers):
    return jnp.where(lax.axis_index("pop") == 0, walkers - 1, 0)


def edge_kernel(chunk_ref, change_ref, outside_ref, other_ref, out_ref, other_wide):
    size, rows, width = out_ref.shape
    walkers = other_ref.shape[1]
    j = jnp.where(lax.axis_index("pop") == 0, size - 1, 0)
    row = walkers - 1 - edge_walker(walkers)
    outside = outside_ref[...] > 0.5
    out_ref[...] = chunk_ref[...]
    for t in range(width // 128):
        lanes = slice(t * 128, t * 128 + 128)
        other_wide[t] = other_ref[:, :, lanes].astype(F32).reshape(rows * walkers, 128)
        picked = other_wide[t, pl.ds(row, rows, stride=walkers), :]
        moved = picked + change_ref[:, lanes]
        kept = chunk_ref[j, :, lanes].astype(F32)
        out_ref[j, :, lanes] = jnp.where(outside, moved, kept).astype(BF16)


def make_children(size, parents, green, delta, chol):
    rows, walkers, width = green.shape
    n = chol.shape[1] // rows
    wide = pltpu.VMEM((width // 128, rows * walkers, 128), F32)
    here = [
        pltpu.with_memory_space_constraint(a, pltpu.HBM) for a in (parents, green, delta, chol)
    ]
    return pl.pallas_call(
        functools.partial(children_kernel, n),
        out_shape=[
            jax.ShapeDtypeStruct((size, rows, width), BF16),
            jax.ShapeDtypeStruct((walkers - size, rows, width), BF16),
            jax.ShapeDtypeStruct(chol.shape, BF16),
            jax.ShapeDtypeStruct((rows, width), F32),
            jax.ShapeDtypeStruct((rows, 128), F32),
        ],
        in_specs=[pl.BlockSpec(memory_space=pltpu.HBM)] * 4,
        out_specs=[VMEM] * 5,
        scratch_shapes=[
            pltpu.SMEM(parents.shape, jnp.int32),
            pltpu.VMEM(green.shape, BF16),
            pltpu.VMEM(delta.shape, BF16),
            wide,
            wide,
            pltpu.SemaphoreType.DMA((3 + n,)),
        ],
        cost_estimate=pl.CostEstimate(
            flops=green.size, bytes_accessed=6 * green.size, transcendentals=0
        ),
        compiler_params=pltpu.CompilerParams(vmem_limit_bytes=8 << 20),
        name="children",
    )(*here)


def finish_edge(chunk, change, outside, other):
    rows, walkers, width = other.shape
    return pl.pallas_call(
        edge_kernel,
        out_shape=jax.ShapeDtypeStruct(chunk.shape, BF16),
        in_specs=[VMEM] * 4,
        out_specs=VMEM,
        scratch_shapes=[pltpu.VMEM((width // 128, rows * walkers, 128), F32)],
        cost_estimate=pl.CostEstimate(
            flops=other.size, bytes_accessed=4 * other.size, transcendentals=0
        ),
        compiler_params=pltpu.CompilerParams(vmem_limit_bytes=4 << 20),
        name="edge",
    )(chunk, change, outside, other)


def force_kernel(energy_scale, n, *refs):
    chol_ref, chunks, outs = refs[0], refs[1 : n + 1], refs[n + 1 : 2 * n + 1]
    low = refs[2 * n + 1]
    size, rows, width = chunks[0].shape
    vectors, orbitals, _ = chol_ref.shape
    terms = vectors * orbitals

    def child(c, lanes):
        return jnp.concatenate([chunks[r][c, :, lanes] for r in range(n)], axis=0)

    for c in range(0, size, 2):
        pair = range(c, min(c + 2, size))
        cross = lax.dot_general(
            chol_ref[...].reshape(terms, width),
            jnp.concatenate([child(w, slice(None)) for w in pair], axis=0),
            (((1,), (1,)), ((), ())),
            preferred_element_type=F32,
        ).astype(BF16)
        for d, w in enumerate(pair):
            for g in range(vectors):
                low[w, :, g * orbitals : (g + 1) * orbitals] = cross[
                    g * orbitals : (g + 1) * orbitals, d * orbitals : (d + 1) * orbitals
                ]
    sums = [jnp.zeros((1, 128), F32)] * size
    span = 256 if width % 256 == 0 else 128
    for first in range(0, width, span):
        force = jnp.dot(
            low[...].reshape(size * orbitals, terms),
            chol_ref[:, :, first : first + span].reshape(terms, span),
            preferred_element_type=F32,
        )
        for c in range(size):
            for lane in range(0, span, 128):
                lanes = slice(first + lane, first + lane + 128)
                block = force[c * orbitals : (c + 1) * orbitals, lane : lane + 128]
                product = child(c, lanes).astype(F32) * block
                sums[c] = sums[c] + jnp.sum(product, axis=0, keepdims=True)
                for r in range(n):
                    place = message_block(c, (first + lane) // 128, rows, width)
                    outs[r][place, :] = block[r * rows : (r + 1) * rows, :].astype(outs[r].dtype)
    sums = jnp.concatenate(sums + [jnp.zeros((8 - size, 128), F32)], axis=0)
    energy = jnp.sum(sums, axis=1, keepdims=True) * energy_scale
    high = energy.astype(BF16).astype(F32)
    lane = lax.broadcasted_iota(jnp.int32, (8, 128), 1) - 2 * lax.axis_index("chol")
    tile = jnp.where(lane == 0, high, 0.0) + jnp.where(lane == 1, energy - high, 0.0)
    for r in range(n):
        outs[r][message_rows(size, rows, width) - 8 :, :] = tile.astype(outs[r].dtype)


def partial_forces(chol, chunks):
    n = len(chunks)
    size, rows, width = chunks[0].shape
    vectors, orbitals, _ = chol.shape
    total = n * vectors
    shape = (message_rows(size, rows, width), 128)
    return pl.pallas_call(
        functools.partial(force_kernel, -0.125 / (total * orbitals), n),
        out_shape=[jax.ShapeDtypeStruct(shape, F32)]
        + [jax.ShapeDtypeStruct(shape, BF16)] * (n - 1),
        in_specs=[VMEM] * (1 + n),
        out_specs=[VMEM] * n,
        scratch_shapes=[
            pltpu.VMEM((size, orbitals, vectors * orbitals), BF16),
        ],
        cost_estimate=pl.CostEstimate(
            flops=4 * size * orbitals * width * vectors * orbitals,
            bytes_accessed=2 * chol.size + 4 * size * orbitals * width,
            transcendentals=0,
        ),
        compiler_params=pltpu.CompilerParams(vmem_limit_bytes=16 << 20),
    )(chol, *chunks)


def parents_kernel(factor, size, parents_ref, counts_ref, edge_ref, *refs):
    groups = (refs[0:3], refs[3:6])
    out_ref, energy_ref, total, spread = refs[6:]
    rows, walkers, width = out_ref.shape
    blocks = width // 128
    mine = lax.axis_index("pop")
    row = lax.broadcasted_iota(jnp.int32, (8, 128), 0)
    lane = lax.broadcasted_iota(jnp.int32, (8, 128), 1)
    energies = jnp.zeros((1, 128), F32)
    for group, (own, up, down) in enumerate(groups):
        base = group_base(group, walkers, size)
        for j in range(size):
            span = slice(j * blocks * rows, (j + 1) * blocks * rows)
            total[base + j] = own[span, :] + up[span, :].astype(F32) + down[span, :].astype(F32)
        tail = slice(size * blocks * rows, size * blocks * rows + 8)
        halves = own[tail, :] + up[tail, :].astype(F32) + down[tail, :].astype(F32)
        column = jnp.sum(halves, axis=1, keepdims=True)
        here = jnp.logical_and(lane == row + base, row < size)
        energies = energies + jnp.sum(jnp.where(here, column, 0.0), axis=0, keepdims=True)
    energy_ref[...] = energies[:, :walkers]
    edge = edge_ref[...].astype(F32)
    last = parents_ref.shape[0] - 1
    for p in range(walkers):
        parent = mine * walkers + p
        summed = jnp.zeros((blocks * rows, 128), F32)
        for c in range(max(p - 1, 0), min(p + 2, walkers)):
            hit = parents_ref[mine * walkers + c] == parent
            summed = summed + jnp.where(hit, total[c], 0.0)
        if p in (0, walkers - 1):
            child = parent + (1 if p else -1)
            valid = jnp.logical_and(child >= 0, child <= last)
            found = parents_ref[jnp.clip(child, 0, last)] == parent
            summed = summed + jnp.where(jnp.logical_and(valid, found), edge, 0.0)
        mean = summed * (factor / jnp.maximum(counts_ref[p], 1).astype(F32))
        for t in range(blocks):
            spread[t, pl.ds(p, rows, stride=walkers), :] = mean[t * rows : (t + 1) * rows, :]
    for t in range(blocks):
        block = spread[t].astype(BF16).reshape(rows, walkers, 128)
        out_ref[:, :, t * 128 : t * 128 + 128] = block


def parent_forces(shape, size, factor, parents, counts, edge, group0, group1):
    rows, walkers, width = shape
    return pl.pallas_call(
        functools.partial(parents_kernel, factor, size),
        out_shape=[
            jax.ShapeDtypeStruct(shape, BF16),
            jax.ShapeDtypeStruct((1, walkers), F32),
        ],
        in_specs=[SMEM, SMEM] + [VMEM] * 7,
        out_specs=[VMEM, VMEM],
        scratch_shapes=[
            pltpu.VMEM((walkers, rows * width // 128, 128), F32),
            pltpu.VMEM((width // 128, rows * walkers, 128), F32),
        ],
        cost_estimate=pl.CostEstimate(
            flops=6 * rows * walkers * width,
            bytes_accessed=10 * rows * walkers * width,
            transcendentals=0,
        ),
        compiler_params=pltpu.CompilerParams(vmem_limit_bytes=6 << 20),
        name="parents",
    )(parents, counts, edge, *group0, *group1)


def swap_cores(x):
    return lax.ppermute(x, "pop", [(0, 1), (1, 0)])


def add_low(own, received):
    return (own.astype(F32) + received.astype(F32)).astype(BF16)


def hop_order(n):
    half = n // 2
    order = []
    for s in range(1, half):
        order += [("gather", s, g, way) for g in (0, 1) for way in ("up", "down")]
    order += [("gather", half, 0, "up"), ("gather", half, 1, "down")]
    order += [("sum", 1, 0, "up"), ("sum", 1, 1, "down")]
    for s in range(1, half):
        order += [("sum", s + 1, 0, "up"), ("sum", s, 0, "down")]
        order += [("sum", s, 1, "up"), ("sum", s + 1, 1, "down")]
    return order


def ring_shards(green_half, step_delta, chol_vectors, copy_counts, parents):
    n = lax.axis_size("chol")
    rows, walkers, width = green_half.shape
    size = walkers // 2
    pairs = {"up": ring_pairs(n, 1), "down": ring_pairs(n, -1)}
    hops = ({"up": n // 2, "down": n // 2 - 1}, {"up": n // 2 - 1, "down": n // 2})

    def hop(x, key):
        return lax.ppermute(x, "chol", pairs[key[3]])

    factor = -1.0 / (n * chol_vectors.shape[0]) ** 0.5

    other = swap_cores(green_half)
    *own, chol, change, outside = make_children(
        size, parents, green_half, step_delta, chol_vectors
    )
    own[0] = finish_edge(own[0], change, outside, other)
    chunks = [[own[g]] + [None] * (n - 1) for g in (0, 1)]
    parts = [None, None]
    arrived = [{}, {}]
    for key in hop_order(n):
        phase, s, g, way = key
        if phase == "gather":
            here, there = (n - s, (n - s + 1) % n) if way == "up" else (s, s - 1)
            chunks[g][here] = hop(chunks[g][there], key)
            continue
        if parts[g] is None:
            parts[g] = partial_forces(chol, chunks[g])
        left = hops[g][way] - s + 1
        send = parts[g][left if way == "up" else n - left]
        if s > 1:
            send = add_low(send, arrived[g][way])
        arrived[g][way] = hop(send, key)

    group0, group1 = [(parts[g][0], arrived[g]["up"], arrived[g]["down"]) for g in (0, 1)]
    per_walker = rows * width // 128
    at = (size - 1) * (1 - lax.axis_index("pop")) * per_walker
    own, up, down = [
        lax.dynamic_slice_in_dim(a, at, per_walker, 0).astype(F32) for a in group0
    ]
    edge = swap_cores((own + up + down).astype(BF16))
    parent_force, energy = parent_forces(
        green_half.shape, size, factor, parents, copy_counts, edge, group0, group1
    )
    return parent_force, energy.reshape(walkers)


def on_ring(n, pops, rows, walkers):
    whole_tiles = rows % 16 == 0 and walkers % 8 == 0 and walkers <= 16
    return whole_tiles and n & (n - 1) == 0 and 4 <= n <= 64 and pops == 2


def shards(green_half, step_delta, chol_vectors, copy_counts, parents):
    rows, walkers, _ = green_half.shape
    if on_ring(lax.axis_size("chol"), lax.axis_size("pop"), rows, walkers):
        return ring_shards(green_half, step_delta, chol_vectors, copy_counts, parents)
    return plain_shards(green_half, step_delta, chol_vectors, copy_counts, parents)


def solution(mesh):
    placed = (
        P(("rep", "chol"), "pop", None),
        P(("rep", "chol"), "pop", None),
        P(("rep", "chol"), None, None),
        P(("rep", "pop")),
        P("rep"),
    )
    step = jax.shard_map(
        shards,
        mesh=mesh,
        in_specs=placed,
        out_specs=(P(("rep", "chol"), "pop", None), P(("rep", "pop"))),
        check_vma=False,
    )

    def run(green_half, step_delta, chol_vectors, copy_counts, parents):
        given = (green_half, step_delta, chol_vectors, copy_counts, parents)
        return step(*given)

    return run
```

```python
import functools

import jax
import jax.numpy as jnp
from jax import lax
from jax.experimental import pallas as pl
from jax.experimental.pallas import tpu as pltpu
from jax.sharding import PartitionSpec as P


F32 = jnp.float32
BF16 = jnp.bfloat16
VMEM = pl.BlockSpec(memory_space=pltpu.VMEM)
SMEM = pl.BlockSpec(memory_space=pltpu.SMEM)


def plain_shards(green_half, step_delta, chol_vectors, copy_counts, parents):
    per_group = green_half.shape[1]
    total_chol = lax.axis_size("chol") * chol_vectors.shape[0]
    orbitals = chol_vectors.shape[1]
    factor = -1.0 / total_chol**0.5
    all_parents = lax.all_gather(green_half, "pop", axis=1, tiled=True)
    my_parents = lax.dynamic_slice_in_dim(parents, lax.axis_index("pop") * per_group, per_group, 0)
    picked = jnp.take(all_parents, my_parents, axis=1)
    child_rows = (picked.astype(F32) + step_delta.astype(F32)).astype(BF16)
    cross = jnp.einsum(
        "iwm,gkm->wgik",
        lax.all_gather(child_rows, "chol", axis=0, tiled=True),
        chol_vectors,
        preferred_element_type=F32,
    )
    cross_low = cross.astype(BF16)
    trace_part = jnp.sum(cross_low.astype(F32) * jnp.swapaxes(cross, 2, 3), axis=(1, 2, 3))
    child_energy = lax.psum(trace_part, "chol") * (-0.125 / (total_chol * orbitals))
    forces = lax.psum_scatter(
        factor * jnp.einsum("wgik,gil->kwl", cross_low, chol_vectors, preferred_element_type=F32),
        "chol",
        scatter_dimension=0,
        tiled=True,
    )
    parent_slots = jnp.arange(all_parents.shape[1], dtype=jnp.int32)
    one_hot = (my_parents[:, None] == parent_slots[None, :]).astype(F32)
    spread_sum = jnp.einsum("kcl,cp->kpl", forces, one_hot, precision=lax.Precision.HIGHEST)
    summed = lax.psum_scatter(
        spread_sum.astype(BF16), "pop", scatter_dimension=1, tiled=True
    ).astype(F32)
    divisor = jnp.maximum(copy_counts, 1).astype(F32)
    return (summed / divisor[None, :, None]).astype(BF16), child_energy


def ring_device(n, place):
    return place * 2 if place < n // 2 else 2 * (n - 1 - place) + 1


def ring_pairs(n, step):
    return [(ring_device(n, q), ring_device(n, (q + step) % n)) for q in range(n)]


def block_at(n, offset):
    me = lax.axis_index("chol")
    place = jnp.where(lax.rem(me, 2) == 0, me // 2, n - 1 - me // 2)
    place = lax.rem(place + offset, n)
    return jnp.where(place < n // 2, 2 * place, 2 * (n - 1 - place) + 1)


def group_base(group, walkers, size):
    first = lax.axis_index("pop") * (walkers - size)
    return (walkers - size) - first if group == 0 else first


def message_rows(size, rows, width):
    return size * rows * (width // 128) + 8


def message_block(c, t, rows, width):
    first = (c * (width // 128) + t) * rows
    return slice(first, first + rows)


def children_kernel(n, parents_any, green_any, delta_any, chol_any, *refs):
    out0_ref, out1_ref, chol_ref, change_ref, outside_ref = refs[:5]
    parents_ref, green_ref, delta_ref, green_wide, delta_wide, sems = refs[5:]
    rows, walkers, width = green_ref.shape
    moves = [(parents_any, parents_ref), (green_any, green_ref), (delta_any, delta_ref)]
    for r in range(n):
        first = pl.multiple_of(block_at(n, r) * rows, rows)
        moves.append(
            (chol_any.at[:, pl.ds(first, rows), :], chol_ref.at[:, pl.ds(r * rows, rows), :])
        )
    copies = [
        pltpu.make_async_copy(source, target, sems.at[k])
        for k, (source, target) in enumerate(moves)
    ]
    for copy in copies:
        copy.start()
    for copy in copies[:3]:
        copy.wait()
    mine = lax.axis_index("pop")
    blocks = [slice(t * 128, t * 128 + 128) for t in range(width // 128)]
    for t, lanes in enumerate(blocks):
        green_wide[t] = green_ref[:, :, lanes].astype(F32).reshape(rows * walkers, 128)
        delta_wide[t] = delta_ref[:, :, lanes].astype(F32).reshape(rows * walkers, 128)

    def local_parent(walker):
        return parents_ref[mine * walkers + walker] - mine * walkers

    for group, out_ref in enumerate((out0_ref, out1_ref)):
        size = out_ref.shape[0]
        base = group_base(group, walkers, size)
        for j in range(size):
            walker = base + j
            source = jnp.clip(local_parent(walker), 0, walkers - 1)
            for t, lanes in enumerate(blocks):
                picked = green_wide[t, pl.ds(source, rows, stride=walkers), :]
                change = delta_wide[t, pl.ds(walker, rows, stride=walkers), :]
                out_ref[j, :, lanes] = (picked + change).astype(BF16)
    child = edge_walker(walkers)
    for t, lanes in enumerate(blocks):
        change_ref[:, lanes] = delta_wide[t, pl.ds(child, rows, stride=walkers), :]
    parent = local_parent(child)
    outside = jnp.where(jnp.logical_or(parent < 0, parent >= walkers), 1.0, 0.0)
    outside_ref[...] = jnp.full((rows, 128), outside, F32)
    for copy in copies[3:]:
        copy.wait()


def edge_walker(walkers):
    return jnp.where(lax.axis_index("pop") == 0, walkers - 1, 0)


def edge_kernel(chunk_ref, change_ref, outside_ref, other_ref, out_ref, other_wide):
    size, rows, width = out_ref.shape
    walkers = other_ref.shape[1]
    j = jnp.where(lax.axis_index("pop") == 0, size - 1, 0)
    row = walkers - 1 - edge_walker(walkers)
    outside = outside_ref[...] > 0.5
    out_ref[...] = chunk_ref[...]
    for t in range(width // 128):
        lanes = slice(t * 128, t * 128 + 128)
        other_wide[t] = other_ref[:, :, lanes].astype(F32).reshape(rows * walkers, 128)
        picked = other_wide[t, pl.ds(row, rows, stride=walkers), :]
        moved = picked + change_ref[:, lanes]
        kept = chunk_ref[j, :, lanes].astype(F32)
        out_ref[j, :, lanes] = jnp.where(outside, moved, kept).astype(BF16)


def make_children(size, parents, green, delta, chol):
    rows, walkers, width = green.shape
    n = chol.shape[1] // rows
    wide = pltpu.VMEM((width // 128, rows * walkers, 128), F32)
    here = [
        pltpu.with_memory_space_constraint(a, pltpu.HBM) for a in (parents, green, delta, chol)
    ]
    return pl.pallas_call(
        functools.partial(children_kernel, n),
        out_shape=[
            jax.ShapeDtypeStruct((size, rows, width), BF16),
            jax.ShapeDtypeStruct((walkers - size, rows, width), BF16),
            jax.ShapeDtypeStruct(chol.shape, BF16),
            jax.ShapeDtypeStruct((rows, width), F32),
            jax.ShapeDtypeStruct((rows, 128), F32),
        ],
        in_specs=[pl.BlockSpec(memory_space=pltpu.HBM)] * 4,
        out_specs=[VMEM] * 5,
        scratch_shapes=[
            pltpu.SMEM(parents.shape, jnp.int32),
            pltpu.VMEM(green.shape, BF16),
            pltpu.VMEM(delta.shape, BF16),
            wide,
            wide,
            pltpu.SemaphoreType.DMA((3 + n,)),
        ],
        cost_estimate=pl.CostEstimate(
            flops=green.size, bytes_accessed=6 * green.size, transcendentals=0
        ),
        compiler_params=pltpu.CompilerParams(vmem_limit_bytes=8 << 20),
        name="children",
    )(*here)


def finish_edge(chunk, change, outside, other):
    rows, walkers, width = other.shape
    return pl.pallas_call(
        edge_kernel,
        out_shape=jax.ShapeDtypeStruct(chunk.shape, BF16),
        in_specs=[VMEM] * 4,
        out_specs=VMEM,
        scratch_shapes=[pltpu.VMEM((width // 128, rows * walkers, 128), F32)],
        cost_estimate=pl.CostEstimate(
            flops=other.size, bytes_accessed=4 * other.size, transcendentals=0
        ),
        compiler_params=pltpu.CompilerParams(vmem_limit_bytes=4 << 20),
        name="edge",
    )(chunk, change, outside, other)


def force_kernel(energy_scale, n, *refs):
    chol_ref, chunks, outs = refs[0], refs[1 : n + 1], refs[n + 1 : 2 * n + 1]
    low = refs[2 * n + 1]
    size, rows, width = chunks[0].shape
    vectors, orbitals, _ = chol_ref.shape
    terms = vectors * orbitals

    def child(c, lanes):
        return jnp.concatenate([chunks[r][c, :, lanes] for r in range(n)], axis=0)

    for c in range(0, size, 2):
        pair = range(c, min(c + 2, size))
        cross = lax.dot_general(
            chol_ref[...].reshape(terms, width),
            jnp.concatenate([child(w, slice(None)) for w in pair], axis=0),
            (((1,), (1,)), ((), ())),
            preferred_element_type=F32,
        ).astype(BF16)
        for d, w in enumerate(pair):
            for g in range(vectors):
                low[w, :, g * orbitals : (g + 1) * orbitals] = cross[
                    g * orbitals : (g + 1) * orbitals, d * orbitals : (d + 1) * orbitals
                ]
    sums = [jnp.zeros((1, 128), F32)] * size
    span = 256 if width % 256 == 0 else 128
    for first in range(0, width, span):
        force = jnp.dot(
            low[...].reshape(size * orbitals, terms),
            chol_ref[:, :, first : first + span].reshape(terms, span),
            preferred_element_type=F32,
        )
        for c in range(size):
            for lane in range(0, span, 128):
                lanes = slice(first + lane, first + lane + 128)
                block = force[c * orbitals : (c + 1) * orbitals, lane : lane + 128]
                product = child(c, lanes).astype(F32) * block
                sums[c] = sums[c] + jnp.sum(product, axis=0, keepdims=True)
                for r in range(n):
                    place = message_block(c, (first + lane) // 128, rows, width)
                    outs[r][place, :] = block[r * rows : (r + 1) * rows, :].astype(outs[r].dtype)
    sums = jnp.concatenate(sums + [jnp.zeros((8 - size, 128), F32)], axis=0)
    energy = jnp.sum(sums, axis=1, keepdims=True) * energy_scale
    high = energy.astype(BF16).astype(F32)
    lane = lax.broadcasted_iota(jnp.int32, (8, 128), 1) - 2 * lax.axis_index("chol")
    tile = jnp.where(lane == 0, high, 0.0) + jnp.where(lane == 1, energy - high, 0.0)
    for r in range(n):
        outs[r][message_rows(size, rows, width) - 8 :, :] = tile.astype(outs[r].dtype)


def partial_forces(chol, chunks):
    n = len(chunks)
    size, rows, width = chunks[0].shape
    vectors, orbitals, _ = chol.shape
    total = n * vectors
    shape = (message_rows(size, rows, width), 128)
    return pl.pallas_call(
        functools.partial(force_kernel, -0.125 / (total * orbitals), n),
        out_shape=[jax.ShapeDtypeStruct(shape, F32)]
        + [jax.ShapeDtypeStruct(shape, BF16)] * (n - 1),
        in_specs=[VMEM] * (1 + n),
        out_specs=[VMEM] * n,
        scratch_shapes=[
            pltpu.VMEM((size, orbitals, vectors * orbitals), BF16),
        ],
        cost_estimate=pl.CostEstimate(
            flops=4 * size * orbitals * width * vectors * orbitals,
            bytes_accessed=2 * chol.size + 4 * size * orbitals * width,
            transcendentals=0,
        ),
        compiler_params=pltpu.CompilerParams(vmem_limit_bytes=16 << 20),
    )(chol, *chunks)


def parents_kernel(factor, size, parents_ref, counts_ref, edge_ref, *refs):
    groups = (refs[0:3], refs[3:6])
    out_ref, energy_ref, total, spread = refs[6:]
    rows, walkers, width = out_ref.shape
    blocks = width // 128
    mine = lax.axis_index("pop")
    row = lax.broadcasted_iota(jnp.int32, (8, 128), 0)
    lane = lax.broadcasted_iota(jnp.int32, (8, 128), 1)
    energies = jnp.zeros((1, 128), F32)
    for group, (own, up, down) in enumerate(groups):
        base = group_base(group, walkers, size)
        for j in range(size):
            span = slice(j * blocks * rows, (j + 1) * blocks * rows)
            total[base + j] = own[span, :] + up[span, :].astype(F32) + down[span, :].astype(F32)
        tail = slice(size * blocks * rows, size * blocks * rows + 8)
        halves = own[tail, :] + up[tail, :].astype(F32) + down[tail, :].astype(F32)
        column = jnp.sum(halves, axis=1, keepdims=True)
        here = jnp.logical_and(lane == row + base, row < size)
        energies = energies + jnp.sum(jnp.where(here, column, 0.0), axis=0, keepdims=True)
    energy_ref[...] = energies[:, :walkers]
    edge = edge_ref[...].astype(F32)
    last = parents_ref.shape[0] - 1
    for p in range(walkers):
        parent = mine * walkers + p
        summed = jnp.zeros((blocks * rows, 128), F32)
        for c in range(max(p - 1, 0), min(p + 2, walkers)):
            hit = parents_ref[mine * walkers + c] == parent
            summed = summed + jnp.where(hit, total[c], 0.0)
        if p in (0, walkers - 1):
            child = parent + (1 if p else -1)
            valid = jnp.logical_and(child >= 0, child <= last)
            found = parents_ref[jnp.clip(child, 0, last)] == parent
            summed = summed + jnp.where(jnp.logical_and(valid, found), edge, 0.0)
        mean = summed * (factor / jnp.maximum(counts_ref[p], 1).astype(F32))
        for t in range(blocks):
            spread[t, pl.ds(p, rows, stride=walkers), :] = mean[t * rows : (t + 1) * rows, :]
    for t in range(blocks):
        block = spread[t].astype(BF16).reshape(rows, walkers, 128)
        out_ref[:, :, t * 128 : t * 128 + 128] = block


def parent_forces(shape, size, factor, parents, counts, edge, group0, group1):
    rows, walkers, width = shape
    return pl.pallas_call(
        functools.partial(parents_kernel, factor, size),
        out_shape=[
            jax.ShapeDtypeStruct(shape, BF16),
            jax.ShapeDtypeStruct((1, walkers), F32),
        ],
        in_specs=[SMEM, SMEM] + [VMEM] * 7,
        out_specs=[VMEM, VMEM],
        scratch_shapes=[
            pltpu.VMEM((walkers, rows * width // 128, 128), F32),
            pltpu.VMEM((width // 128, rows * walkers, 128), F32),
        ],
        cost_estimate=pl.CostEstimate(
            flops=6 * rows * walkers * width,
            bytes_accessed=10 * rows * walkers * width,
            transcendentals=0,
        ),
        compiler_params=pltpu.CompilerParams(vmem_limit_bytes=6 << 20),
        name="parents",
    )(parents, counts, edge, *group0, *group1)


def swap_cores(x):
    return lax.ppermute(x, "pop", [(0, 1), (1, 0)])


def add_low(own, received):
    return (own.astype(F32) + received.astype(F32)).astype(BF16)


def hop_order(n):
    half = n // 2
    order = []
    for s in range(1, half):
        order += [("gather", s, g, way) for g in (0, 1) for way in ("up", "down")]
    order += [("gather", half, 0, "up"), ("gather", half, 1, "down")]
    for s in range(1, half):
        order += [("sum", s, 0, "up"), ("sum", s, 1, "down")]
        order += [("sum", s, 1, "up"), ("sum", s, 0, "down")]
    order += [("sum", half, 0, "up"), ("sum", half, 1, "down")]
    return order


def ring_shards(green_half, step_delta, chol_vectors, copy_counts, parents):
    n = lax.axis_size("chol")
    rows, walkers, width = green_half.shape
    size = walkers // 2
    pairs = {"up": ring_pairs(n, 1), "down": ring_pairs(n, -1)}
    hops = ({"up": n // 2, "down": n // 2 - 1}, {"up": n // 2 - 1, "down": n // 2})

    def hop(x, key):
        return lax.ppermute(x, "chol", pairs[key[3]])

    factor = -1.0 / (n * chol_vectors.shape[0]) ** 0.5

    other = swap_cores(green_half)
    *own, chol, change, outside = make_children(
        size, parents, green_half, step_delta, chol_vectors
    )
    own[0] = finish_edge(own[0], change, outside, other)
    chunks = [[own[g]] + [None] * (n - 1) for g in (0, 1)]
    parts = [None, None]
    arrived = [{}, {}]
    for key in hop_order(n):
        phase, s, g, way = key
        if phase == "gather":
            here, there = (n - s, (n - s + 1) % n) if way == "up" else (s, s - 1)
            chunks[g][here] = hop(chunks[g][there], key)
            continue
        if parts[g] is None:
            parts[g] = partial_forces(chol, chunks[g])
        left = hops[g][way] - s + 1
        send = parts[g][left if way == "up" else n - left]
        if s > 1:
            send = add_low(send, arrived[g][way])
        arrived[g][way] = hop(send, key)

    group0, group1 = [(parts[g][0], arrived[g]["up"], arrived[g]["down"]) for g in (0, 1)]
    per_walker = rows * width // 128
    at = (size - 1) * (1 - lax.axis_index("pop")) * per_walker
    own, up, down = [
        lax.dynamic_slice_in_dim(a, at, per_walker, 0).astype(F32) for a in group0
    ]
    edge = swap_cores((own + up + down).astype(BF16))
    parent_force, energy = parent_forces(
        green_half.shape, size, factor, parents, copy_counts, edge, group0, group1
    )
    return parent_force, energy.reshape(walkers)


def on_ring(n, pops, rows, walkers):
    whole_tiles = rows % 16 == 0 and walkers % 8 == 0 and walkers <= 16
    return whole_tiles and n & (n - 1) == 0 and 4 <= n <= 64 and pops == 2


def shards(green_half, step_delta, chol_vectors, copy_counts, parents):
    rows, walkers, _ = green_half.shape
    if on_ring(lax.axis_size("chol"), lax.axis_size("pop"), rows, walkers):
        return ring_shards(green_half, step_delta, chol_vectors, copy_counts, parents)
    return plain_shards(green_half, step_delta, chol_vectors, copy_counts, parents)


def solution(mesh):
    placed = (
        P(("rep", "chol"), "pop", None),
        P(("rep", "chol"), "pop", None),
        P(("rep", "chol"), None, None),
        P(("rep", "pop")),
        P("rep"),
    )
    step = jax.shard_map(
        shards,
        mesh=mesh,
        in_specs=placed,
        out_specs=(P(("rep", "chol"), "pop", None), P(("rep", "pop"))),
        check_vma=False,
    )

    def run(green_half, step_delta, chol_vectors, copy_counts, parents):
        given = (green_half, step_delta, chol_vectors, copy_counts, parents)
        return step(*given)

    return run
```

```python
import functools

import jax
import jax.numpy as jnp
from jax import lax
from jax.experimental import pallas as pl
from jax.experimental.pallas import tpu as pltpu
from jax.sharding import PartitionSpec as P


F32 = jnp.float32
BF16 = jnp.bfloat16
VMEM = pl.BlockSpec(memory_space=pltpu.VMEM)
SMEM = pl.BlockSpec(memory_space=pltpu.SMEM)


def plain_shards(green_half, step_delta, chol_vectors, copy_counts, parents):
    per_group = green_half.shape[1]
    total_chol = lax.axis_size("chol") * chol_vectors.shape[0]
    orbitals = chol_vectors.shape[1]
    factor = -1.0 / total_chol**0.5
    all_parents = lax.all_gather(green_half, "pop", axis=1, tiled=True)
    my_parents = lax.dynamic_slice_in_dim(parents, lax.axis_index("pop") * per_group, per_group, 0)
    picked = jnp.take(all_parents, my_parents, axis=1)
    child_rows = (picked.astype(F32) + step_delta.astype(F32)).astype(BF16)
    cross = jnp.einsum(
        "iwm,gkm->wgik",
        lax.all_gather(child_rows, "chol", axis=0, tiled=True),
        chol_vectors,
        preferred_element_type=F32,
    )
    cross_low = cross.astype(BF16)
    trace_part = jnp.sum(cross_low.astype(F32) * jnp.swapaxes(cross, 2, 3), axis=(1, 2, 3))
    child_energy = lax.psum(trace_part, "chol") * (-0.125 / (total_chol * orbitals))
    forces = lax.psum_scatter(
        factor * jnp.einsum("wgik,gil->kwl", cross_low, chol_vectors, preferred_element_type=F32),
        "chol",
        scatter_dimension=0,
        tiled=True,
    )
    parent_slots = jnp.arange(all_parents.shape[1], dtype=jnp.int32)
    one_hot = (my_parents[:, None] == parent_slots[None, :]).astype(F32)
    spread_sum = jnp.einsum("kcl,cp->kpl", forces, one_hot, precision=lax.Precision.HIGHEST)
    summed = lax.psum_scatter(
        spread_sum.astype(BF16), "pop", scatter_dimension=1, tiled=True
    ).astype(F32)
    divisor = jnp.maximum(copy_counts, 1).astype(F32)
    return (summed / divisor[None, :, None]).astype(BF16), child_energy


def ring_device(n, place):
    return place * 2 if place < n // 2 else 2 * (n - 1 - place) + 1


def ring_pairs(n, step):
    return [(ring_device(n, q), ring_device(n, (q + step) % n)) for q in range(n)]


def block_at(n, offset):
    me = lax.axis_index("chol")
    place = jnp.where(lax.rem(me, 2) == 0, me // 2, n - 1 - me // 2)
    place = lax.rem(place + offset, n)
    return jnp.where(place < n // 2, 2 * place, 2 * (n - 1 - place) + 1)


def group_base(group, walkers, size):
    first = lax.axis_index("pop") * (walkers - size)
    return (walkers - size) - first if group == 0 else first


def message_rows(size, rows, width):
    return size * rows * (width // 128) + 8


def message_block(c, t, rows, width):
    first = (c * (width // 128) + t) * rows
    return slice(first, first + rows)


def children_kernel(n, parents_any, green_any, delta_any, chol_any, *refs):
    out0_ref, out1_ref, chol_ref, change_ref, outside_ref = refs[:5]
    parents_ref, green_ref, delta_ref, green_wide, delta_wide, sems = refs[5:]
    rows, walkers, width = green_ref.shape
    moves = [(parents_any, parents_ref), (green_any, green_ref), (delta_any, delta_ref)]
    for r in range(n):
        first = pl.multiple_of(block_at(n, r) * rows, rows)
        moves.append(
            (chol_any.at[:, pl.ds(first, rows), :], chol_ref.at[:, pl.ds(r * rows, rows), :])
        )
    copies = [
        pltpu.make_async_copy(source, target, sems.at[k])
        for k, (source, target) in enumerate(moves)
    ]
    for copy in copies:
        copy.start()
    for copy in copies[:3]:
        copy.wait()
    mine = lax.axis_index("pop")
    blocks = [slice(t * 128, t * 128 + 128) for t in range(width // 128)]
    for t, lanes in enumerate(blocks):
        green_wide[t] = green_ref[:, :, lanes].astype(F32).reshape(rows * walkers, 128)
        delta_wide[t] = delta_ref[:, :, lanes].astype(F32).reshape(rows * walkers, 128)

    def local_parent(walker):
        return parents_ref[mine * walkers + walker] - mine * walkers

    for group, out_ref in enumerate((out0_ref, out1_ref)):
        size = out_ref.shape[0]
        base = group_base(group, walkers, size)
        for j in range(size):
            walker = base + j
            source = jnp.clip(local_parent(walker), 0, walkers - 1)
            for t, lanes in enumerate(blocks):
                picked = green_wide[t, pl.ds(source, rows, stride=walkers), :]
                change = delta_wide[t, pl.ds(walker, rows, stride=walkers), :]
                out_ref[j, :, lanes] = (picked + change).astype(BF16)
    child = edge_walker(walkers)
    for t, lanes in enumerate(blocks):
        change_ref[:, lanes] = delta_wide[t, pl.ds(child, rows, stride=walkers), :]
    parent = local_parent(child)
    outside = jnp.where(jnp.logical_or(parent < 0, parent >= walkers), 1.0, 0.0)
    outside_ref[...] = jnp.full((rows, 128), outside, F32)
    for copy in copies[3:]:
        copy.wait()


def edge_walker(walkers):
    return jnp.where(lax.axis_index("pop") == 0, walkers - 1, 0)


def edge_kernel(chunk_ref, change_ref, outside_ref, other_ref, out_ref, other_wide):
    size, rows, width = out_ref.shape
    walkers = other_ref.shape[1]
    j = jnp.where(lax.axis_index("pop") == 0, size - 1, 0)
    row = walkers - 1 - edge_walker(walkers)
    outside = outside_ref[...] > 0.5
    out_ref[...] = chunk_ref[...]
    for t in range(width // 128):
        lanes = slice(t * 128, t * 128 + 128)
        other_wide[t] = other_ref[:, :, lanes].astype(F32).reshape(rows * walkers, 128)
        picked = other_wide[t, pl.ds(row, rows, stride=walkers), :]
        moved = picked + change_ref[:, lanes]
        kept = chunk_ref[j, :, lanes].astype(F32)
        out_ref[j, :, lanes] = jnp.where(outside, moved, kept).astype(BF16)


def make_children(size, parents, green, delta, chol):
    rows, walkers, width = green.shape
    n = chol.shape[1] // rows
    wide = pltpu.VMEM((width // 128, rows * walkers, 128), F32)
    here = [
        pltpu.with_memory_space_constraint(a, pltpu.HBM) for a in (parents, green, delta, chol)
    ]
    return pl.pallas_call(
        functools.partial(children_kernel, n),
        out_shape=[
            jax.ShapeDtypeStruct((size, rows, width), BF16),
            jax.ShapeDtypeStruct((walkers - size, rows, width), BF16),
            jax.ShapeDtypeStruct(chol.shape, BF16),
            jax.ShapeDtypeStruct((rows, width), F32),
            jax.ShapeDtypeStruct((rows, 128), F32),
        ],
        in_specs=[pl.BlockSpec(memory_space=pltpu.HBM)] * 4,
        out_specs=[VMEM] * 5,
        scratch_shapes=[
            pltpu.SMEM(parents.shape, jnp.int32),
            pltpu.VMEM(green.shape, BF16),
            pltpu.VMEM(delta.shape, BF16),
            wide,
            wide,
            pltpu.SemaphoreType.DMA((3 + n,)),
        ],
        cost_estimate=pl.CostEstimate(
            flops=green.size, bytes_accessed=6 * green.size, transcendentals=0
        ),
        compiler_params=pltpu.CompilerParams(vmem_limit_bytes=8 << 20),
        name="children",
    )(*here)


def finish_edge(chunk, change, outside, other):
    rows, walkers, width = other.shape
    return pl.pallas_call(
        edge_kernel,
        out_shape=jax.ShapeDtypeStruct(chunk.shape, BF16),
        in_specs=[VMEM] * 4,
        out_specs=VMEM,
        scratch_shapes=[pltpu.VMEM((width // 128, rows * walkers, 128), F32)],
        cost_estimate=pl.CostEstimate(
            flops=other.size, bytes_accessed=4 * other.size, transcendentals=0
        ),
        compiler_params=pltpu.CompilerParams(vmem_limit_bytes=4 << 20),
        name="edge",
    )(chunk, change, outside, other)


def force_kernel(energy_scale, n, *refs):
    chol_ref, chunks, outs = refs[0], refs[1 : n + 1], refs[n + 1 : 2 * n + 1]
    low = refs[2 * n + 1]
    size, rows, width = chunks[0].shape
    vectors, orbitals, _ = chol_ref.shape
    terms = vectors * orbitals

    def child(c, lanes):
        return jnp.concatenate([chunks[r][c, :, lanes] for r in range(n)], axis=0)

    for c in range(0, size, 2):
        pair = range(c, min(c + 2, size))
        cross = lax.dot_general(
            chol_ref[...].reshape(terms, width),
            jnp.concatenate([child(w, slice(None)) for w in pair], axis=0),
            (((1,), (1,)), ((), ())),
            preferred_element_type=F32,
        ).astype(BF16)
        for d, w in enumerate(pair):
            for g in range(vectors):
                low[w, :, g * orbitals : (g + 1) * orbitals] = cross[
                    g * orbitals : (g + 1) * orbitals, d * orbitals : (d + 1) * orbitals
                ]
    sums = [jnp.zeros((1, 128), F32)] * size
    span = 256 if width % 256 == 0 else 128
    for first in range(0, width, span):
        force = jnp.dot(
            low[...].reshape(size * orbitals, terms),
            chol_ref[:, :, first : first + span].reshape(terms, span),
            preferred_element_type=F32,
        )
        for c in range(size):
            for lane in range(0, span, 128):
                lanes = slice(first + lane, first + lane + 128)
                block = force[c * orbitals : (c + 1) * orbitals, lane : lane + 128]
                product = child(c, lanes).astype(F32) * block
                sums[c] = sums[c] + jnp.sum(product, axis=0, keepdims=True)
                for r in range(n):
                    place = message_block(c, (first + lane) // 128, rows, width)
                    outs[r][place, :] = block[r * rows : (r + 1) * rows, :].astype(outs[r].dtype)
    sums = jnp.concatenate(sums + [jnp.zeros((8 - size, 128), F32)], axis=0)
    energy = jnp.sum(sums, axis=1, keepdims=True) * energy_scale
    high = energy.astype(BF16).astype(F32)
    lane = lax.broadcasted_iota(jnp.int32, (8, 128), 1) - 2 * lax.axis_index("chol")
    tile = jnp.where(lane == 0, high, 0.0) + jnp.where(lane == 1, energy - high, 0.0)
    for r in range(n):
        outs[r][message_rows(size, rows, width) - 8 :, :] = tile.astype(outs[r].dtype)


def partial_forces(chol, chunks):
    n = len(chunks)
    size, rows, width = chunks[0].shape
    vectors, orbitals, _ = chol.shape
    total = n * vectors
    shape = (message_rows(size, rows, width), 128)
    return pl.pallas_call(
        functools.partial(force_kernel, -0.125 / (total * orbitals), n),
        out_shape=[jax.ShapeDtypeStruct(shape, F32)]
        + [jax.ShapeDtypeStruct(shape, BF16)] * (n - 1),
        in_specs=[VMEM] * (1 + n),
        out_specs=[VMEM] * n,
        scratch_shapes=[
            pltpu.VMEM((size, orbitals, vectors * orbitals), BF16),
        ],
        cost_estimate=pl.CostEstimate(
            flops=4 * size * orbitals * width * vectors * orbitals,
            bytes_accessed=2 * chol.size + 4 * size * orbitals * width,
            transcendentals=0,
        ),
        compiler_params=pltpu.CompilerParams(vmem_limit_bytes=16 << 20),
    )(chol, *chunks)


def parents_kernel(factor, size, parents_ref, counts_ref, edge_ref, *refs):
    groups = (refs[0:3], refs[3:6])
    out_ref, energy_ref, total, spread = refs[6:]
    rows, walkers, width = out_ref.shape
    mine = lax.axis_index("pop")
    last = parents_ref.shape[0] - 1
    hits, edge_hits, scales = {}, {}, []
    for p in range(walkers):
        parent = mine * walkers + p
        for c in range(max(p - 1, 0), min(p + 2, walkers)):
            hits[c, p] = parents_ref[mine * walkers + c] == parent
        if p in (0, walkers - 1):
            child = parent + (1 if p else -1)
            valid = jnp.logical_and(child >= 0, child <= last)
            found = parents_ref[jnp.clip(child, 0, last)] == parent
            edge_hits[p] = jnp.logical_and(valid, found)
        scales.append(factor / jnp.maximum(counts_ref[p], 1).astype(F32))
    for t in range(width // 128):
        for group, (own, up, down) in enumerate(groups):
            base = group_base(group, walkers, size)
            for j in range(size):
                place = message_block(j, t, rows, width)
                total[t, base + j] = (
                    own[place, :] + up[place, :].astype(F32) + down[place, :].astype(F32)
                )
        edge = edge_ref[t * rows : (t + 1) * rows, :].astype(F32)
        for p in range(walkers):
            summed = jnp.zeros((rows, 128), F32)
            for c in range(max(p - 1, 0), min(p + 2, walkers)):
                summed = summed + jnp.where(hits[c, p], total[t, c], 0.0)
            if p in edge_hits:
                summed = summed + jnp.where(edge_hits[p], edge, 0.0)
            spread[t, pl.ds(p, rows, stride=walkers), :] = summed * scales[p]
        lanes = slice(t * 128, t * 128 + 128)
        out_ref[:, :, lanes] = spread[t].astype(BF16).reshape(rows, walkers, 128)
    row = lax.broadcasted_iota(jnp.int32, (8, 128), 0)
    lane = lax.broadcasted_iota(jnp.int32, (8, 128), 1)
    energies = jnp.zeros((1, 128), F32)
    for group, (own, up, down) in enumerate(groups):
        tail = slice(message_rows(size, rows, width) - 8, message_rows(size, rows, width))
        halves = own[tail, :] + up[tail, :].astype(F32) + down[tail, :].astype(F32)
        column = jnp.sum(halves, axis=1, keepdims=True)
        here = jnp.logical_and(lane == row + group_base(group, walkers, size), row < size)
        energies = energies + jnp.sum(jnp.where(here, column, 0.0), axis=0, keepdims=True)
    energy_ref[...] = energies[:, :walkers]


def parent_forces(shape, size, factor, parents, counts, edge, group0, group1):
    rows, walkers, width = shape
    blocks = width // 128
    return pl.pallas_call(
        functools.partial(parents_kernel, factor, size),
        out_shape=[
            jax.ShapeDtypeStruct(shape, BF16),
            jax.ShapeDtypeStruct((1, walkers), F32),
        ],
        in_specs=[SMEM, SMEM] + [VMEM] * 7,
        out_specs=[VMEM, VMEM],
        scratch_shapes=[
            pltpu.VMEM((blocks, walkers, rows, 128), F32),
            pltpu.VMEM((blocks, rows * walkers, 128), F32),
        ],
        cost_estimate=pl.CostEstimate(
            flops=6 * rows * walkers * width,
            bytes_accessed=10 * rows * walkers * width,
            transcendentals=0,
        ),
        compiler_params=pltpu.CompilerParams(vmem_limit_bytes=6 << 20),
        name="parents",
    )(parents, counts, edge, *group0, *group1)


def swap_cores(x):
    return lax.ppermute(x, "pop", [(0, 1), (1, 0)])


def add_low(own, received):
    return (own.astype(F32) + received.astype(F32)).astype(BF16)


def hop_order(n):
    half = n // 2
    order = []
    for s in range(1, half):
        order += [("gather", s, g, way) for g in (0, 1) for way in ("up", "down")]
    order += [("gather", half, 0, "up"), ("gather", half, 1, "down")]
    for s in range(1, half):
        order += [("sum", s, 0, "up"), ("sum", s, 1, "down")]
        order += [("sum", s, 1, "up"), ("sum", s, 0, "down")]
    order += [("sum", half, 0, "up"), ("sum", half, 1, "down")]
    return order


def ring_shards(green_half, step_delta, chol_vectors, copy_counts, parents):
    n = lax.axis_size("chol")
    rows, walkers, width = green_half.shape
    size = walkers // 2
    pairs = {"up": ring_pairs(n, 1), "down": ring_pairs(n, -1)}
    hops = ({"up": n // 2, "down": n // 2 - 1}, {"up": n // 2 - 1, "down": n // 2})

    def hop(x, key):
        return lax.ppermute(x, "chol", pairs[key[3]])

    factor = -1.0 / (n * chol_vectors.shape[0]) ** 0.5

    other = swap_cores(green_half)
    *own, chol, change, outside = make_children(
        size, parents, green_half, step_delta, chol_vectors
    )
    own[0] = finish_edge(own[0], change, outside, other)
    chunks = [[own[g]] + [None] * (n - 1) for g in (0, 1)]
    parts = [None, None]
    arrived = [{}, {}]
    for key in hop_order(n):
        phase, s, g, way = key
        if phase == "gather":
            here, there = (n - s, (n - s + 1) % n) if way == "up" else (s, s - 1)
            chunks[g][here] = hop(chunks[g][there], key)
            continue
        if parts[g] is None:
            parts[g] = partial_forces(chol, chunks[g])
        left = hops[g][way] - s + 1
        send = parts[g][left if way == "up" else n - left]
        if s > 1:
            send = add_low(send, arrived[g][way])
        arrived[g][way] = hop(send, key)

    group0, group1 = [(parts[g][0], arrived[g]["up"], arrived[g]["down"]) for g in (0, 1)]
    per_walker = rows * width // 128
    at = (size - 1) * (1 - lax.axis_index("pop")) * per_walker
    own, up, down = [
        lax.dynamic_slice_in_dim(a, at, per_walker, 0).astype(F32) for a in group0
    ]
    edge = swap_cores((own + up + down).astype(BF16))
    parent_force, energy = parent_forces(
        green_half.shape, size, factor, parents, copy_counts, edge, group0, group1
    )
    return parent_force, energy.reshape(walkers)


def on_ring(n, pops, rows, walkers):
    whole_tiles = rows % 16 == 0 and walkers % 8 == 0 and walkers <= 16
    return whole_tiles and n & (n - 1) == 0 and 4 <= n <= 64 and pops == 2


def shards(green_half, step_delta, chol_vectors, copy_counts, parents):
    rows, walkers, _ = green_half.shape
    if on_ring(lax.axis_size("chol"), lax.axis_size("pop"), rows, walkers):
        return ring_shards(green_half, step_delta, chol_vectors, copy_counts, parents)
    return plain_shards(green_half, step_delta, chol_vectors, copy_counts, parents)


def solution(mesh):
    placed = (
        P(("rep", "chol"), "pop", None),
        P(("rep", "chol"), "pop", None),
        P(("rep", "chol"), None, None),
        P(("rep", "pop")),
        P("rep"),
    )
    step = jax.shard_map(
        shards,
        mesh=mesh,
        in_specs=placed,
        out_specs=(P(("rep", "chol"), "pop", None), P(("rep", "pop"))),
        check_vma=False,
    )

    def run(green_half, step_delta, chol_vectors, copy_counts, parents):
        given = (green_half, step_delta, chol_vectors, copy_counts, parents)
        return step(*given)

    return run
```
